256 devices in a mesh: row: 8 (over z_lo, y), col: 32 (over z_hi, x, core).
Axes of the slice: x: 4, y: 4, z: 8 (z_hi: 4, z_lo: 2; z = z_hi * 2 + z_lo), core: 2. Of those that a mesh axis runs over, the one named last changes fastest.
Arguments:
- points: float32 [16, 32768], P(None, ('row', 'col')), may hold values from -6 to 6
- inverse_length: float32 [16], replicated, may hold values from 0.35 to 1.4
- target: float32 [32768], P(('row', 'col')), may hold values from -6 to 6
- probe_bits: int32 [15, 32768], P(None, ('row', 'col')), may hold values from 0 to 1
- leaf_inverse: float32 [32768, 128], P(('row', 'col')), may hold values from -1 to 4, as said below
- top_basis: float32 [64, 32768], P(None, ('row', 'col')), may hold values from -0.09375 to 0.09375
- sub_basis: float32 [64, 32768], P(None, ('row', 'col')), may hold values from -0.1875 to 0.1875
Outputs:
- solution: float32 [16, 32768], P(None, ('row', 'col'))
- residual: float32 [16, 32768], P(None, ('row', 'col'))
- coefficients: float32 [2, 2, 16], replicated
The draws below stay inside these ranges and needn't reach their ends.
Inputs may be any that keep to these rules, and one draw needn't show every extreme that they name: `leaf_inverse`: each leaf block is symmetric, and each of its diagonal entries exceeds the sum of the absolute values of the other entries of its row.
All inputs are finite; a program needn't handle non-finite values.
Results may differ from the reference program's by a relative error of at most 0.0003.
Values sent between devices are 32-bit elements; how exact they have to be, the bound alone decides.
No kernel may reach another device: no remote copies, remote signals or barrier semaphores. Data moves between devices by JAX's collectives and lax.ppermute only.
A program may use at most 64 MiB of HBM per device.

```python
import math
import jax
import jax.numpy as jnp
from jax import lax

DIM = 16
RANK = 64
PROBES = 15
ITERS = 2
PTS_DEV = 128
NPTS = 32768
N_ROW = 8
N_COL = 32


def draw_leaf_inverse(key, part):
    nleaf = NPTS // PTS_DEV
    key_off = jax.random.fold_in(key, 11)
    key_diag = jax.random.fold_in(key, 12)
    raw = jax.random.uniform(key_off, (nleaf, PTS_DEV, PTS_DEV), jnp.float32, -1.0, 1.0) * (0.7 / PTS_DEV)
    sym = 0.5 * (raw + raw.transpose(0, 2, 1))
    eye = jnp.eye(PTS_DEV, dtype=jnp.float32)
    diag = jax.random.uniform(key_diag, (nleaf, PTS_DEV), jnp.float32, 0.8, 1.6)
    full = sym * (1.0 - eye)[None] + diag[:, :, None] * eye[None]
    return full.reshape(NPTS, PTS_DEV)


def set_ends(array, rng, low, top_value):
    longest = array.shape.index(max(array.shape))
    spots = []
    for shift in (0, 1):
        where = [jax.random.randint(jax.random.fold_in(rng, axis), (), 0, length) for axis, length in enumerate(array.shape)]
        where[longest] = (where[longest] + shift) % array.shape[longest]
        spots.append(tuple(where))
    return array.at[spots[0]].set(low).at[spots[1]].set(top_value)


def block_levels(own_key, extent, shards, low, largest):
    factor_of = 1.0
    for axis_at, shards_of in shards:
        heights = jax.random.uniform(jax.random.fold_in(jax.random.fold_in(own_key, 6), axis_at), (shards_of,), jnp.float32, low / len(shards), largest / len(shards))
        factor_of = factor_of * jnp.repeat(jnp.exp(heights), extent[axis_at] // shards_of).reshape((-1,) + (1,) * (len(extent) - 1 - axis_at))
    return factor_of


def gaussian(rng, extent, spread, reach, shards=(), kind=jnp.bfloat16):
    drawn = spread * jax.random.normal(rng, extent, jnp.float32)
    if shards:
        drawn = drawn * block_levels(rng, extent, shards, -0.22, 0.18)
    return jnp.clip(drawn, -reach, reach).astype(kind)


def setup_inputs(seed: int = 0) -> dict:
    splits = jax.random.split(jax.random.key(seed), 8)
    points = gaussian(splits[0], (DIM, NPTS), 1.0, 6.0, ((1, 256),), jnp.float32)
    inverse_length = jnp.clip(jnp.exp(jax.random.uniform(splits[1], (DIM,), jnp.float32, math.log(0.35), math.log(1.4))), 0.35, 1.4)
    target = gaussian(splits[2], (NPTS,), 1.0, 6.0, ((0, 256),), jnp.float32)
    probe_bits = set_ends(jax.random.randint(splits[3], (PROBES, NPTS), 0, 2), jax.random.fold_in(splits[3], 1), 0, 1).astype(jnp.int32)
    leaf_inverse = draw_leaf_inverse(jax.random.fold_in(splits[7], 71), 0)
    top_basis = gaussian(splits[5], (RANK, NPTS), (NPTS // 8) ** -0.5, 0.09375, ((1, 256),), jnp.float32)
    sub_basis = gaussian(splits[6], (RANK, NPTS), (PTS_DEV * N_COL // 4) ** -0.5, 0.1875, ((1, 256),), jnp.float32)
    return {"points": points, "inverse_length": inverse_length, "target": target, "probe_bits": probe_bits, "leaf_inverse": leaf_inverse, "top_basis": top_basis, "sub_basis": sub_basis}


root_five = math.sqrt(5.0)
noise_level = 0.5

def matern_block(left, right):
    left_sq = lax.optimization_barrier(jnp.sum(left * left, 0))
    right_sq = lax.optimization_barrier(jnp.sum(right * right, 0))
    cross = lax.dot_general(left, right, (((0,), (0,)), ((), ())), precision=lax.Precision.HIGHEST, preferred_element_type=jnp.float32)
    dist_sq = jnp.maximum(left_sq[:, None] + right_sq[None, :] - 2.0 * cross, 0.0)
    dist = jnp.sqrt(dist_sq)
    return (1.0 + root_five * dist + 5.0 / 3.0 * dist_sq) * jnp.exp(-root_five * dist)

def apply_kernel(scaled, vectors):
    blocks = scaled.reshape(scaled.shape[0], NPTS // PTS_DEV, PTS_DEV).transpose(1, 0, 2)

    def one_block(block_pts):
        kmat = matern_block(scaled, block_pts)
        return jnp.dot(vectors, kmat, precision=lax.Precision.HIGHEST, preferred_element_type=jnp.float32)
    out = lax.map(one_block, blocks)
    return out.transpose(1, 0, 2).reshape(vectors.shape) + noise_level * vectors

def apply_precond(vectors, leaf_inverse, top_basis, sub_basis):
    cols = vectors.shape[0]
    nleaf = NPTS // PTS_DEV
    leaves = leaf_inverse.reshape(nleaf, PTS_DEV, PTS_DEV)
    pieces = vectors.reshape(cols, nleaf, PTS_DEV)
    result = jnp.einsum('blm,cbm->cbl', leaves, pieces, precision=lax.Precision.HIGHEST).reshape(cols, NPTS)
    top_coef = jnp.dot(top_basis, vectors.T, precision=lax.Precision.HIGHEST, preferred_element_type=jnp.float32)
    result = result + jnp.dot(top_coef.T, top_basis, precision=lax.Precision.HIGHEST, preferred_element_type=jnp.float32)
    sub_view = sub_basis.reshape(RANK, N_ROW, NPTS // N_ROW)
    vec_view = vectors.reshape(cols, N_ROW, NPTS // N_ROW)
    sub_coef = jnp.einsum('knm,cnm->nkc', sub_view, vec_view, precision=lax.Precision.HIGHEST)
    result = result + jnp.einsum('nkc,knm->cnm', sub_coef, sub_view, precision=lax.Precision.HIGHEST).reshape(cols, NPTS)
    return result

def reference(points, inverse_length, target, probe_bits, leaf_inverse, top_basis, sub_basis):
    scaled = points * inverse_length[:, None]
    signs = 2.0 * probe_bits.astype(jnp.float32) - 1.0
    rhs = jnp.concatenate([target[None, :], signs], axis=0)
    solution = jnp.zeros_like(rhs)
    residual = rhs
    precond = apply_precond(residual, leaf_inverse, top_basis, sub_basis)
    direction = precond
    rz_now = lax.optimization_barrier(jnp.sum(residual * precond, 1))
    alphas = []
    betas = []
    for step in range(ITERS):
        image = apply_kernel(scaled, direction)
        alpha = rz_now / lax.optimization_barrier(jnp.sum(direction * image, 1))
        solution = solution + alpha[:, None] * direction
        residual = residual - alpha[:, None] * image
        precond = apply_precond(residual, leaf_inverse, top_basis, sub_basis)
        rz_next = lax.optimization_barrier(jnp.sum(residual * precond, 1))
        beta = rz_next / rz_now
        direction = precond + beta[:, None] * direction
        rz_now = rz_next
        alphas.append(alpha)
        betas.append(beta)
    coefficients = jnp.stack([jnp.stack(alphas), jnp.stack(betas)])
    return (solution, residual, coefficients)
```

```python
import functools
import math

import jax
import jax.numpy as jnp
from jax import lax
from jax.experimental import pallas as pl
from jax.experimental.pallas import tpu as pltpu
from jax.sharding import Mesh
from jax.sharding import PartitionSpec as P

AXES = ("zl", "y", "zh", "x", "c")
G1 = ("zh", "x")
G2 = ("zl", "y", "c")
NG = 16
NT = 8
COLS = 16
PTS = 128
RANK = 64
NOISE = 0.5
F32 = jnp.float32
BF16 = jnp.bfloat16
LN2 = math.log(2.0)
COORD_SCALE = math.sqrt(5.0) / LN2
HIGHEST = lax.Precision.HIGHEST


def dot_nt(a, b):
    return lax.dot_general(a, b, (((1,), (1,)), ((), ())), precision=HIGHEST, preferred_element_type=F32)


def dot_nn(a, b):
    return lax.dot_general(a, b, (((1,), (0,)), ((), ())), precision=HIGHEST, preferred_element_type=F32)


def lane(shape):
    return lax.broadcasted_iota(jnp.int32, shape, 1)


def sublane(shape):
    return lax.broadcasted_iota(jnp.int32, shape, 0)


def pack(sums):
    shape = (COLS, PTS)
    acc = jnp.zeros(shape, F32)
    for k, s in enumerate(sums):
        acc = jnp.where(lane(shape) == COLS * k + sublane(shape), jnp.broadcast_to(s, shape), acc)
    return jnp.sum(acc, 0, keepdims=True)


def unpack(row, k):
    shape = (COLS, PTS)
    hit = lane(shape) == COLS * k + sublane(shape)
    return jnp.sum(jnp.where(hit, jnp.broadcast_to(row, shape), 0.0), 1, keepdims=True)


def rowdot(a, b):
    return jnp.sum(a * b, 1, keepdims=True)


def tile_rows(rows):
    shape = (8, PTS)
    out = jnp.zeros(shape, F32)
    for k, r in enumerate(rows):
        out = jnp.where(sublane(shape) == k, jnp.broadcast_to(r, shape), out)
    return out


def tree_sum(terms):
    terms = list(terms)
    while len(terms) > 1:
        terms = [terms[i] + terms[i + 1] if i + 1 < len(terms) else terms[i] for i in range(0, len(terms), 2)]
    return terms[0]


def call(kernel, outs, *args, smem=0, limit=8 << 20, scratch=(), name=None):
    specs = [pl.BlockSpec(memory_space=pltpu.SMEM)] * smem
    specs += [pl.BlockSpec(memory_space=pltpu.VMEM)] * (len(args) - smem)
    return pl.pallas_call(
        kernel,
        out_shape=[jax.ShapeDtypeStruct(s, d) for s, d in outs],
        in_specs=specs,
        out_specs=[pl.BlockSpec(memory_space=pltpu.VMEM)] * len(outs),
        scratch_shapes=list(scratch),
        compiler_params=pltpu.CompilerParams(vmem_limit_bytes=limit),
        name=name,
    )(*args)


def start_kernel(points, inv, target, bits, top, sub, send, rhs, basis):
    rhs[0:1, :] = target[...]
    rhs[1:COLS, :] = 2.0 * bits[...].astype(F32) - 1.0
    basis[0:RANK, :] = top[...]
    basis[RANK : 2 * RANK, :] = sub[...]
    send[0:COLS, :] = points[...] * inv[...]
    send[COLS : 2 * COLS, :] = dot_nt(rhs[...], basis[...])


def fold_kernel(keep, got, own, send):
    send[...] = tree_sum([got[j] for j in range(NG)])
    if keep:
        send[0:keep, :] = own[0:keep, :]


def subtree_table(got, first, table):
    for t in range(NT):
        table[t] = got[2 * t, first : first + COLS] + got[2 * t + 1, first : first + COLS]


def own_coefs(table, mine):
    top = lane((COLS, PTS)) < RANK
    return tree_sum([jnp.where(top | (mine == t), table[t], 0.0) for t in range(NT)])


def precond0_kernel(tid, got, rhs, leaf, basis, z, table):
    subtree_table(got, COLS, table)
    coefs = own_coefs(table, tid[0])
    z[...] = dot_nt(rhs[...], leaf[...]) + dot_nn(coefs, basis[...])


def features(x, left):
    def pieces(v):
        first = v.astype(BF16).astype(F32)
        second = (v - first).astype(BF16).astype(F32)
        third = (v - first - second).astype(BF16).astype(F32)
        return first, second, third

    a, b, c = pieces(x)
    norms = pieces(jnp.sum(x * x, 0, keepdims=True))
    ones = (jnp.ones((1, PTS), F32),) * 3
    if left:
        parts = [a, a, b, b, a, c]
        tail = tile_rows(norms + ones)
    else:
        a, b, c = -2.0 * a, -2.0 * b, -2.0 * c
        parts = [a, b, a, b, c, a]
        tail = tile_rows(ones + norms)
    return jnp.concatenate(parts + [tail, jnp.zeros((PTS - 6 * COLS - 8, PTS), F32)], 0)


def matern_kernel(left, right, high, low, left_f, right_f):
    for j in range(NG):
        at = slice(j * PTS, (j + 1) * PTS)
        right_f[:, at] = features(right[j, 0:COLS] * COORD_SCALE, False).astype(BF16)
        left_f[at, :] = features(left[j, 0:COLS] * COORD_SCALE, True).T.astype(BF16)
    width = 256

    def step(i, carry):
        rows = pl.ds(pl.multiple_of(i * PTS, PTS), PTS)
        lhs = left_f[rows, :]
        for j in range(0, NG * PTS, width):
            s = jnp.dot(lhs, right_f[:, j : j + width], preferred_element_type=F32)
            s = jnp.maximum(s, 1e-30)
            v = s * lax.rsqrt(s)
            k = ((LN2 * LN2 / 3.0 * s + 1.0) + LN2 * v) * jnp.exp2(-v)
            h = k.astype(BF16)
            high[rows, j : j + width] = h
            low[rows, j : j + width] = (k - h.astype(F32)).astype(BF16)
        return carry

    lax.fori_loop(0, NG, step, 0)


def matvec_kernel(got, high, low, out):
    v = jnp.concatenate([got[j] for j in range(NG)], 1)
    v_high = v.astype(BF16)
    both = jnp.concatenate([v_high, (v - v_high.astype(F32)).astype(BF16)], 0)
    width = 512
    for j in range(0, NG * PTS, width):
        r = jnp.dot(both, high[:, j : j + width], preferred_element_type=F32)
        r = r[0:COLS] + r[COLS:] + jnp.dot(v_high, low[:, j : j + width], preferred_element_type=F32)
        for b in range(width // PTS):
            out[j // PTS + b] = r[:, b * PTS : (b + 1) * PTS]


def image0_kernel(got, z, rhs, basis, q, send):
    q[...] = tree_sum([got[j] for j in range(NG)]) + NOISE * z[...]
    send[0:COLS, :] = dot_nt(q[...], basis[...])
    send[COLS:, :] = tile_rows([pack([rowdot(rhs[...], z[...]), rowdot(z[...], q[...])])])


def precond1_kernel(tid, got, rhs, q, leaf, basis, table0, z, res, table, table_q, sums):
    sums[...] = tree_sum([got[j, COLS:] for j in range(NG)])
    alpha = unpack(sums[0:1, :], 0) / unpack(sums[0:1, :], 1)
    subtree_table(got, 0, table_q)
    for t in range(NT):
        table[t] = table0[t] - alpha * table_q[t]
    coefs = own_coefs(table, tid[0])
    res[...] = rhs[...] - alpha * q[...]
    z[...] = dot_nt(res[...], leaf[...]) + dot_nn(coefs, basis[...])


def image1_kernel(got, z1, z0, res, q, leaf, basis, p, send):
    p[...] = tree_sum([got[j] for j in range(NG)]) + NOISE * z1[...]
    send[0:COLS, :] = dot_nt(p[...], basis[...])
    rv, qv, pv, zv = res[...], q[...], p[...], z1[...]
    rb, qb, pb = (dot_nt(v, leaf[...]) for v in (rv, qv, pv))
    first = pack([rowdot(rv, zv), rowdot(zv, pv), rowdot(zv, qv), rowdot(z0[...], pv)])
    second = pack([rowdot(rv, rb), rowdot(rv, qb), rowdot(rv, pb), rowdot(qv, qb), rowdot(qv, pb), rowdot(pv, pb)])
    send[COLS:, :] = tile_rows([first, second])


def finish_kernel(got, z0, z1, res, q, p, table1, table_q, sums0, x_out, r_out, coefs):
    sums = tree_sum([got[j, COLS:] for j in range(NG)])
    rz0, z0q = unpack(sums0[0:1, :], 0), unpack(sums0[0:1, :], 1)
    rz1, z1p, z1q, z0p = (unpack(sums[0:1, :], k) for k in range(4))
    rbr, rbq, rbp, qbq, qbp, pbp = (unpack(sums[1:2, :], k) for k in range(6))
    alpha0 = rz0 / z0q
    beta0 = rz1 / rz0
    alpha1 = rz1 / (z1p + beta0 * (z1q + z0p) + beta0 * beta0 * z0q)
    image = p[...] + beta0 * q[...]
    r_out[...] = res[...] - alpha1 * image
    x_out[...] = alpha0 * z0[...] + alpha1 * (z1[...] + beta0 * z0[...])
    leaf_part = (
        rbr
        - 2.0 * alpha1 * (rbp + beta0 * rbq)
        + alpha1 * alpha1 * (pbp + 2.0 * beta0 * qbp + beta0 * beta0 * qbq)
    )
    top = lane((COLS, PTS)) < RANK
    now = [
        table1[t] - alpha1 * (got[2 * t, 0:COLS] + got[2 * t + 1, 0:COLS] + beta0 * table_q[t]) for t in range(NT)
    ]
    whole = jnp.where(top, tree_sum(now), 0.0)
    squares = whole * whole + tree_sum([jnp.where(top, 0.0, v * v) for v in now])
    beta1 = (leaf_part + jnp.sum(squares, 1, keepdims=True)) / rz1
    for k, v in enumerate((alpha0, alpha1, beta0, beta1)):
        coefs[k // 2, k % 2 : k % 2 + 1, :] = pack([v])[:, 0:COLS]


def gather(block, axes):
    return lax.all_to_all(jnp.broadcast_to(block[None], (NG,) + block.shape), axes, 0, 0, tiled=True)


def on_device(points, inverse_length, target, probe_bits, leaf, top_basis, sub_basis):
    vec = ((COLS, PTS), F32)
    table = ((NT, COLS, PTS), F32)
    block = ((NG * PTS, NG * PTS), BF16)
    tid = lax.axis_index(("zl", "y")).astype(jnp.int32).reshape(1)
    send, rhs, basis = call(
        start_kernel,
        [((2 * COLS, PTS), F32), vec, ((2 * RANK, PTS), F32)],
        points, inverse_length[:, None], target[None, :], probe_bits, top_basis, sub_basis,
        name="start",
    )
    got1 = gather(send, G1)
    (send,) = call(functools.partial(fold_kernel, COLS), [((2 * COLS, PTS), F32)], got1, send, name="fold0")
    got2 = gather(send, G2)
    z0, table0 = call(precond0_kernel, [vec, table], tid, got2, rhs, leaf, basis, smem=1, name="precond0")
    dirs = gather(z0, G1)
    high, low = call(
        matern_kernel, [block, block], got1, got2,
        limit=24 << 20,
        scratch=[pltpu.VMEM((NG * PTS, PTS), BF16), pltpu.VMEM((PTS, NG * PTS), BF16)],
        name="matern",
    )

    def matvec(dirs):
        (parts,) = call(matvec_kernel, [((NG, COLS, PTS), F32)], dirs, high, low, limit=24 << 20, name="matvec")
        return lax.all_to_all(parts, G2, 0, 0, tiled=True)

    wide = ((COLS + 8, PTS), F32)
    q, send = call(image0_kernel, [vec, wide], matvec(dirs), z0, rhs, basis, name="image0")
    (send,) = call(functools.partial(fold_kernel, 0), [wide], gather(send, G1), send, name="fold1")
    z1, res, table1, table_q, sums0 = call(
        precond1_kernel, [vec, vec, table, table, ((8, PTS), F32)],
        tid, gather(send, G2), rhs, q, leaf, basis, table0, smem=1, name="precond1",
    )
    p, send = call(
        image1_kernel, [vec, wide], matvec(gather(z1, G1)), z1, z0, res, q, leaf, basis, name="image1"
    )
    (send,) = call(functools.partial(fold_kernel, 0), [wide], gather(send, G1), send, name="fold2")
    x_out, r_out, coefs = call(
        finish_kernel, [vec, vec, ((2, 2, COLS), F32)],
        gather(send, G2), z0, z1, res, q, p, table1, table_q, sums0, name="finish",
    )
    return x_out, r_out, coefs


def solution(mesh):
    named = Mesh(mesh.devices.reshape(2, 4, 4, 4, 2), AXES)
    return jax.shard_map(
        on_device,
        mesh=named,
        in_specs=(P(None, AXES), P(), P(AXES), P(None, AXES), P(AXES, None), P(None, AXES), P(None, AXES)),
        out_specs=(P(None, AXES), P(None, AXES), P()),
        check_vma=False,
    )
```

```python
import functools
import math

import jax
import jax.numpy as jnp
from jax import lax
from jax.experimental import pallas as pl
from jax.experimental.pallas import tpu as pltpu
from jax.sharding import Mesh
from jax.sharding import PartitionSpec as P

AXES = ("zl", "y", "zh", "x", "c")
G1 = ("zh", "x")
G2 = ("zl", "y", "c")
NG = 16
NT = 8
FIRST = 10
COLS = 16
PTS = 128
RANK = 64
NOISE = 0.5
F32 = jnp.float32
BF16 = jnp.bfloat16
LN2 = math.log(2.0)
COORD_SCALE = math.sqrt(5.0) / LN2
HIGHEST = lax.Precision.HIGHEST


def dot_nt(a, b):
    return lax.dot_general(a, b, (((1,), (1,)), ((), ())), precision=HIGHEST, preferred_element_type=F32)


def dot_nn(a, b):
    return lax.dot_general(a, b, (((1,), (0,)), ((), ())), precision=HIGHEST, preferred_element_type=F32)


def lane(shape):
    return lax.broadcasted_iota(jnp.int32, shape, 1)


def sublane(shape):
    return lax.broadcasted_iota(jnp.int32, shape, 0)


def pack(sums):
    shape = (COLS, PTS)
    acc = jnp.zeros(shape, F32)
    for k, s in enumerate(sums):
        acc = jnp.where(lane(shape) == COLS * k + sublane(shape), jnp.broadcast_to(s, shape), acc)
    return jnp.sum(acc, 0, keepdims=True)


def unpack(row, k):
    shape = (COLS, PTS)
    hit = lane(shape) == COLS * k + sublane(shape)
    return jnp.sum(jnp.where(hit, jnp.broadcast_to(row, shape), 0.0), 1, keepdims=True)


def rowdot(a, b):
    return jnp.sum(a * b, 1, keepdims=True)


def tile_rows(rows):
    shape = (8, PTS)
    out = jnp.zeros(shape, F32)
    for k, r in enumerate(rows):
        out = jnp.where(sublane(shape) == k, jnp.broadcast_to(r, shape), out)
    return out


def tree_sum(terms):
    terms = list(terms)
    while len(terms) > 1:
        terms = [terms[i] + terms[i + 1] if i + 1 < len(terms) else terms[i] for i in range(0, len(terms), 2)]
    return terms[0]


VMEM = pltpu.MemorySpace.VMEM
SMEM = pltpu.MemorySpace.SMEM
HBM = pltpu.MemorySpace.HBM


def call(kernel, outs, *args, spaces=None, out_spaces=None, limit=8 << 20, scratch=(), name=None):
    spaces = spaces or [VMEM] * len(args)
    out_spaces = out_spaces or [VMEM] * len(outs)
    args = [pltpu.with_memory_space_constraint(a, m) if m is HBM else a for a, m in zip(args, spaces)]
    return pl.pallas_call(
        kernel,
        out_shape=[m(s, d) if m is HBM else jax.ShapeDtypeStruct(s, d) for m, (s, d) in zip(out_spaces, outs)],
        in_specs=[pl.BlockSpec(memory_space=m) for m in spaces],
        out_specs=[pl.BlockSpec(memory_space=m) for m in out_spaces],
        scratch_shapes=list(scratch),
        compiler_params=pltpu.CompilerParams(vmem_limit_bytes=limit),
        name=name,
    )(*args)


def start_kernel(tid, inv_h, points_h, target_h, bits_h, top_h, sub_h, leaf_h, send, rhs, basis, leaf, weights, points, target, bits, inv, sems):
    moves = [
        pltpu.make_async_copy(src, dst, sems.at[k])
        for k, (src, dst) in enumerate(
            [
                (bits_h, bits),
                (target_h, target),
                (top_h, basis.at[pl.ds(0, RANK)]),
                (sub_h, basis.at[pl.ds(RANK, RANK)]),
                (points_h, points),
                (inv_h, inv),
                (leaf_h, leaf),
            ]
        )
    ]
    for m in moves:
        m.start()
    mine = (lane((NT, PTS)) < RANK) | (sublane((NT, PTS)) == tid[0])
    weights[...] = jnp.where(mine, 1.0, 0.0)
    for m in moves:
        m.wait()
    scale = jnp.zeros((COLS, PTS), F32)
    for k in range(COLS):
        scale = jnp.where(sublane((COLS, PTS)) == k, inv[k], scale)
    rhs[0:1, :] = target[...]
    rhs[1:COLS, :] = 2.0 * bits[...].astype(F32) - 1.0
    send[0:COLS, :] = points[...] * scale
    send[COLS : 2 * COLS, :] = dot_nt(rhs[...], basis[...])


def fold_kernel(keep, got, own, send):
    send[...] = tree_sum([got[j] for j in range(NG)])
    if keep:
        send[0:keep, :] = own[0:keep, :]


def subtree_table(got, first, table):
    for t in range(NT):
        table[t] = got[2 * t, first : first + COLS] + got[2 * t + 1, first : first + COLS]


def own_coefs(table, weights):
    return tree_sum([table[t] * weights[t : t + 1, :] for t in range(NT)])


def precond0_kernel(got, rhs, leaf, basis, weights, z, table):
    subtree_table(got, COLS, table)
    coefs = own_coefs(table, weights)
    z[...] = dot_nt(rhs[...], leaf[...]) + dot_nn(coefs, basis[...])


def features(x, left):
    def pieces(v):
        first = v.astype(BF16).astype(F32)
        second = (v - first).astype(BF16).astype(F32)
        third = (v - first - second).astype(BF16).astype(F32)
        return first, second, third

    a, b, c = pieces(x)
    norms = pieces(jnp.sum(x * x, 0, keepdims=True))
    ones = (jnp.ones((1, PTS), F32),) * 3
    if left:
        parts = [a, a, b, b, a, c]
        tail = tile_rows(norms + ones)
    else:
        a, b, c = -2.0 * a, -2.0 * b, -2.0 * c
        parts = [a, b, a, b, c, a]
        tail = tile_rows(ones + norms)
    return jnp.concatenate(parts + [tail, jnp.zeros((PTS - 6 * COLS - 8, PTS), F32)], 0)


def matern_rows(lhs, right_f, high, low):
    width = 256
    for j in range(0, NG * PTS, width):
        s = jnp.dot(lhs, right_f[:, j : j + width], preferred_element_type=F32)
        s = jnp.maximum(s, 1e-30)
        v = s * lax.rsqrt(s)
        k = ((LN2 * LN2 / 3.0 * s + 1.0) + LN2 * v) * jnp.exp2(-v)
        h = k.astype(BF16)
        high[:, j : j + width] = h
        low[:, j : j + width] = (k - h.astype(F32)).astype(BF16)


def slab(i):
    return pl.ds(pl.multiple_of(i * PTS, PTS), PTS)


def matern_first_kernel(left, right, high_h, low_h, left_f, right_f, high, low, sems):
    for j in range(NG):
        at = slice(j * PTS, (j + 1) * PTS)
        right_f[:, at] = features(right[j, 0:COLS] * COORD_SCALE, False).astype(BF16)
        left_f[at, :] = features(left[j, 0:COLS] * COORD_SCALE, True).T.astype(BF16)

    def moves(i, slot):
        return (
            pltpu.make_async_copy(high.at[slot], high_h.at[slab(i)], sems.at[slot, 0]),
            pltpu.make_async_copy(low.at[slot], low_h.at[slab(i)], sems.at[slot, 1]),
        )

    def step(i, carry):
        slot = i % 2

        @pl.when(i >= 2)
        def _():
            for m in moves(i - 2, slot):
                m.wait()

        matern_rows(left_f[slab(i), :], right_f, high.at[slot], low.at[slot])
        for m in moves(i, slot):
            m.start()
        return carry

    lax.fori_loop(0, FIRST, step, 0)
    for i in (FIRST - 2, FIRST - 1):
        for m in moves(i, i % 2):
            m.wait()


def matvec_rows(got, high, low, out):
    v = jnp.concatenate([got[j] for j in range(NG)], 1)
    v_high = v.astype(BF16)
    both = jnp.concatenate([v_high, (v - v_high.astype(F32)).astype(BF16)], 0)
    width = 512
    for j in range(0, NG * PTS, width):
        r = jnp.dot(both, high[:, j : j + width], preferred_element_type=F32)
        r = r[0:COLS] + r[COLS:] + jnp.dot(v_high, low[:, j : j + width], preferred_element_type=F32)
        for b in range(width // PTS):
            out[j // PTS + b] = r[:, b * PTS : (b + 1) * PTS]


def matern_rest_kernel(got, left_f, right_f, high_h, low_h, out, high, low, sems):
    done = pl.ds(0, FIRST * PTS)
    moves = (
        pltpu.make_async_copy(high_h, high.at[done], sems.at[0]),
        pltpu.make_async_copy(low_h, low.at[done], sems.at[1]),
    )
    for m in moves:
        m.start()

    def step(i, carry):
        matern_rows(left_f[slab(i), :], right_f, high.at[slab(i)], low.at[slab(i)])
        return carry

    lax.fori_loop(FIRST, NG, step, 0)
    for m in moves:
        m.wait()
    matvec_rows(got, high, low, out)


def image0_kernel(got, z, rhs, basis, q, send):
    q[...] = tree_sum([got[j] for j in range(NG)]) + NOISE * z[...]
    send[0:COLS, :] = dot_nt(q[...], basis[...])
    send[COLS:, :] = tile_rows([pack([rowdot(rhs[...], z[...]), rowdot(z[...], q[...])])])


def precond1_kernel(got, rhs, q, leaf, basis, weights, table0, z, res, table, table_q, sums):
    sums[...] = tree_sum([got[j, COLS:] for j in range(NG)])
    alpha = unpack(sums[0:1, :], 0) / unpack(sums[0:1, :], 1)
    subtree_table(got, 0, table_q)
    for t in range(NT):
        table[t] = table0[t] - alpha * table_q[t]
    coefs = own_coefs(table, weights)
    res[...] = rhs[...] - alpha * q[...]
    z[...] = dot_nt(res[...], leaf[...]) + dot_nn(coefs, basis[...])


def image1_kernel(got, z1, z0, res, q, leaf, basis, p, send):
    p[...] = tree_sum([got[j] for j in range(NG)]) + NOISE * z1[...]
    send[0:COLS, :] = dot_nt(p[...], basis[...])
    rv, qv, pv, zv = res[...], q[...], p[...], z1[...]
    rb, qb, pb = (dot_nt(v, leaf[...]) for v in (rv, qv, pv))
    first = pack([rowdot(rv, zv), rowdot(zv, pv), rowdot(zv, qv), rowdot(z0[...], pv)])
    second = pack([rowdot(rv, rb), rowdot(rv, qb), rowdot(rv, pb), rowdot(qv, qb), rowdot(qv, pb), rowdot(pv, pb)])
    send[COLS:, :] = tile_rows([first, second])


def finish_kernel(got, z0, z1, res, q, p, table1, table_q, sums0, x_out, r_out, coefs):
    sums = tree_sum([got[j, COLS:] for j in range(NG)])
    rz0, z0q = unpack(sums0[0:1, :], 0), unpack(sums0[0:1, :], 1)
    rz1, z1p, z1q, z0p = (unpack(sums[0:1, :], k) for k in range(4))
    rbr, rbq, rbp, qbq, qbp, pbp = (unpack(sums[1:2, :], k) for k in range(6))
    alpha0 = rz0 / z0q
    beta0 = rz1 / rz0
    alpha1 = rz1 / (z1p + beta0 * (z1q + z0p) + beta0 * beta0 * z0q)
    image = p[...] + beta0 * q[...]
    r_out[...] = res[...] - alpha1 * image
    x_out[...] = alpha0 * z0[...] + alpha1 * (z1[...] + beta0 * z0[...])
    leaf_part = (
        rbr
        - 2.0 * alpha1 * (rbp + beta0 * rbq)
        + alpha1 * alpha1 * (pbp + 2.0 * beta0 * qbp + beta0 * beta0 * qbq)
    )
    top = lane((COLS, PTS)) < RANK
    now = [
        table1[t] - alpha1 * (got[2 * t, 0:COLS] + got[2 * t + 1, 0:COLS] + beta0 * table_q[t]) for t in range(NT)
    ]
    whole = jnp.where(top, tree_sum(now), 0.0)
    squares = whole * whole + tree_sum([jnp.where(top, 0.0, v * v) for v in now])
    beta1 = (leaf_part + jnp.sum(squares, 1, keepdims=True)) / rz1
    for k, v in enumerate((alpha0, alpha1, beta0, beta1)):
        coefs[k // 2, k % 2 : k % 2 + 1, :] = pack([v])[:, 0:COLS]


def gather(block, axes):
    return lax.all_to_all(jnp.broadcast_to(block[None], (NG,) + block.shape), axes, 0, 0, tiled=True)


def scatter(parts):
    return lax.all_to_all(parts, G2, 0, 0, tiled=True)


def on_device(points, inverse_length, target, probe_bits, leaf_inverse, top_basis, sub_basis):
    vec = ((COLS, PTS), F32)
    square = ((PTS, PTS), F32)
    table = ((NT, COLS, PTS), F32)
    part = ((FIRST * PTS, NG * PTS), BF16)
    block = ((NG * PTS, NG * PTS), BF16)
    parts = ((NG, COLS, PTS), F32)
    double = ((2 * COLS, PTS), F32)
    wide = ((COLS + 8, PTS), F32)
    dma = pltpu.SemaphoreType.DMA
    tid = lax.axis_index(("zl", "y")).astype(jnp.int32).reshape(1)
    send, rhs, basis, leaf, weights = call(
        start_kernel,
        [double, vec, square, square, ((NT, PTS), F32)],
        tid, inverse_length, points, target[None, :], probe_bits, top_basis, sub_basis, leaf_inverse,
        spaces=[SMEM] + [HBM] * 7,
        scratch=[
            pltpu.VMEM((COLS, PTS), F32), pltpu.VMEM((1, PTS), F32), pltpu.VMEM((COLS - 1, PTS), jnp.int32),
            pltpu.SMEM((COLS,), F32), dma((7,)),
        ],
        name="start",
    )
    got1 = gather(send, G1)
    (send,) = call(functools.partial(fold_kernel, COLS), [double], got1, send, name="fold0")
    got2 = gather(send, G2)
    z0, table0 = call(precond0_kernel, [vec, table], got2, rhs, leaf, basis, weights, name="precond0")
    dirs = gather(z0, G1)
    high_h, low_h, left_f, right_f = call(
        matern_first_kernel, [part, part, ((NG * PTS, PTS), BF16), ((PTS, NG * PTS), BF16)], got1, got2,
        out_spaces=[HBM, HBM, VMEM, VMEM],
        scratch=[pltpu.VMEM((2, PTS, NG * PTS), BF16), pltpu.VMEM((2, PTS, NG * PTS), BF16), dma((2, 2))],
        name="matern_first",
    )
    out, high, low = call(
        matern_rest_kernel, [parts, block, block], dirs, left_f, right_f, high_h, low_h,
        spaces=[VMEM] * 3 + [HBM] * 2, limit=24 << 20, scratch=[dma((2,))], name="matern_rest",
    )
    q, send = call(image0_kernel, [vec, wide], scatter(out), z0, rhs, basis, name="image0")
    (send,) = call(functools.partial(fold_kernel, 0), [wide], gather(send, G1), send, name="fold1")
    z1, res, table1, table_q, sums0 = call(
        precond1_kernel, [vec, vec, table, table, ((8, PTS), F32)],
        gather(send, G2), rhs, q, leaf, basis, weights, table0, name="precond1",
    )
    (out,) = call(matvec_rows, [parts], gather(z1, G1), high, low, limit=24 << 20, name="matvec")
    p, send = call(image1_kernel, [vec, wide], scatter(out), z1, z0, res, q, leaf, basis, name="image1")
    (send,) = call(functools.partial(fold_kernel, 0), [wide], gather(send, G1), send, name="fold2")
    x_out, r_out, coefs = call(
        finish_kernel, [vec, vec, ((2, 2, COLS), F32)],
        gather(send, G2), z0, z1, res, q, p, table1, table_q, sums0, name="finish",
    )
    return x_out, r_out, coefs


def solution(mesh):
    named = Mesh(mesh.devices.reshape(2, 4, 4, 4, 2), AXES)
    return jax.shard_map(
        on_device,
        mesh=named,
        in_specs=(P(None, AXES), P(), P(AXES), P(None, AXES), P(AXES, None), P(None, AXES), P(None, AXES)),
        out_specs=(P(None, AXES), P(None, AXES), P()),
        check_vma=False,
    )
```

```python
import functools
import math

import jax
import jax.numpy as jnp
from jax import lax
from jax.experimental import pallas as pl
from jax.experimental.pallas import tpu as pltpu
from jax.sharding import Mesh
from jax.sharding import PartitionSpec as P

AXES = ("zl", "y", "zh", "x", "c")
GA = ("y", "x")
GB = ("zl", "zh", "c")
NG = 16
NT = 8
COLS = 16
PTS = 128
RANK = 64
NOISE = 0.5
F32 = jnp.float32
BF16 = jnp.bfloat16
LN2 = math.log(2.0)
COORD_SCALE = math.sqrt(5.0) / LN2
HIGHEST = lax.Precision.HIGHEST


def dot_nt(a, b):
    return lax.dot_general(a, b, (((1,), (1,)), ((), ())), precision=HIGHEST, preferred_element_type=F32)


def dot_nn(a, b):
    return lax.dot_general(a, b, (((1,), (0,)), ((), ())), precision=HIGHEST, preferred_element_type=F32)


def lane(shape):
    return lax.broadcasted_iota(jnp.int32, shape, 1)


def sublane(shape):
    return lax.broadcasted_iota(jnp.int32, shape, 0)


def pack(sums):
    shape = (COLS, PTS)
    acc = jnp.zeros(shape, F32)
    for k, s in enumerate(sums):
        acc = jnp.where(lane(shape) == COLS * k + sublane(shape), jnp.broadcast_to(s, shape), acc)
    return jnp.sum(acc, 0, keepdims=True)


def unpack(row, k):
    shape = (COLS, PTS)
    hit = lane(shape) == COLS * k + sublane(shape)
    return jnp.sum(jnp.where(hit, jnp.broadcast_to(row, shape), 0.0), 1, keepdims=True)


def rowdot(a, b):
    return jnp.sum(a * b, 1, keepdims=True)


def tile_rows(rows):
    shape = (8, PTS)
    out = jnp.zeros(shape, F32)
    for k, r in enumerate(rows):
        out = jnp.where(sublane(shape) == k, jnp.broadcast_to(r, shape), out)
    return out


def tree_sum(terms):
    terms = list(terms)
    while len(terms) > 1:
        terms = [terms[i] + terms[i + 1] if i + 1 < len(terms) else terms[i] for i in range(0, len(terms), 2)]
    return terms[0]


VMEM = pltpu.MemorySpace.VMEM
SMEM = pltpu.MemorySpace.SMEM
HBM = pltpu.MemorySpace.HBM


def call(kernel, outs, *args, spaces=None, out_spaces=None, limit=8 << 20, scratch=(), name=None):
    spaces = spaces or [VMEM] * len(args)
    out_spaces = out_spaces or [VMEM] * len(outs)
    args = [pltpu.with_memory_space_constraint(a, m) if m is HBM else a for a, m in zip(args, spaces)]
    return pl.pallas_call(
        kernel,
        out_shape=[m(s, d) if m is HBM else jax.ShapeDtypeStruct(s, d) for m, (s, d) in zip(out_spaces, outs)],
        in_specs=[pl.BlockSpec(memory_space=m) for m in spaces],
        out_specs=[pl.BlockSpec(memory_space=m) for m in out_spaces],
        scratch_shapes=list(scratch),
        compiler_params=pltpu.CompilerParams(vmem_limit_bytes=limit),
        name=name,
    )(*args)


SEND0 = 12 * COLS
BASES = slice(3 * COLS, 3 * COLS + PTS)
LEAF_PART = slice(11 * COLS, 12 * COLS)


def start_kernel(where, inv_h, points_h, target_h, bits_h, top_h, sub_h, leaf_h, send, rhs, basis, leaf, leaf_part, marks, points, target, bits, inv, sems):
    moves = [
        pltpu.make_async_copy(src, dst, sems.at[k])
        for k, (src, dst) in enumerate(
            [
                (bits_h, bits),
                (target_h, target),
                (top_h, basis.at[pl.ds(0, RANK)]),
                (sub_h, basis.at[pl.ds(RANK, RANK)]),
                (points_h, points),
                (inv_h, inv),
                (leaf_h, leaf),
            ]
        )
    ]
    for m in moves:
        m.start()
    row = sublane((NG + 8, PTS))
    place = where[0]
    hit = (row == lax.rem(place, NG)) | ((row >= NG) & (place >= NG))
    marks[...] = jnp.where(hit, 1.0, 0.0)
    for m in moves:
        m.wait()
    scale = jnp.zeros((COLS, PTS), F32)
    for k in range(COLS):
        scale = jnp.where(sublane((COLS, PTS)) == k, inv[k], scale)
    rhs[0:1, :] = target[...]
    rhs[1:COLS, :] = 2.0 * bits[...].astype(F32) - 1.0
    send[0:COLS, :] = points[...] * scale
    send[COLS : 2 * COLS, :] = dot_nt(rhs[...], basis[...])
    leaf_part[...] = dot_nt(rhs[...], leaf[...])


def fold_tiles(got, first, scalars, send, at):
    low = lane((COLS, PTS)) < RANK
    zero = tree_sum([got[j, first : first + COLS] for j in range(NG // 2)])
    one = tree_sum([got[j, first : first + COLS] for j in range(NG // 2, NG)])
    send[at : at + COLS, :] = jnp.where(low, zero + one, zero)
    send[at + COLS : at + 2 * COLS, :] = jnp.where(low, 0.0, one)
    if scalars:
        own = tree_sum([got[j, scalars : scalars + 8] for j in range(NG)])
        send[at + COLS : at + COLS + 8, :] = jnp.where(low[0:8], own, one[0:8])


def fold0_kernel(got, own, basis, leaf_part, send):
    send[0:COLS, :] = own[0:COLS, :]
    fold_tiles(got, COLS, 0, send, COLS)
    send[BASES, :] = basis[...]
    send[LEAF_PART, :] = leaf_part[...]


def fold1_kernel(got, leaf_part, send):
    fold_tiles(got, 0, COLS, send, 0)
    send[2 * COLS : 3 * COLS, :] = leaf_part[...]


def fold2_kernel(got, send):
    fold_tiles(got, 0, COLS, send, 0)


def sum_tiles(got, first):
    return [
        tree_sum([got[4 * y + x, at : at + COLS] for x in range(4)]) for at in (first, first + COLS) for y in range(4)
    ]


def column_directions(marks, table, leaf_parts, got0, directions):
    low = lane((COLS, PTS)) < RANK
    odd = marks[NG : NG + 1, :] > 0.5
    top = tree_sum(table[0:4])
    for y in range(4):
        coefs = jnp.where(low, top, jnp.where(odd, table[4 + y], table[y]))
        high = coefs.astype(BF16)
        both = jnp.concatenate([high, (coefs - high.astype(F32)).astype(BF16)], 0)
        for j in range(4 * y, 4 * y + 4):
            bases = got0[j, BASES]
            first = bases.astype(BF16)
            r = jnp.dot(both, first, preferred_element_type=F32)
            r = r[0:COLS] + r[COLS:] + jnp.dot(high, (bases - first.astype(F32)).astype(BF16), preferred_element_type=F32)
            directions[j] = leaf_parts(j) + r


def own_direction(marks, directions):
    return tree_sum([directions[j] * marks[j : j + 1, :] for j in range(NG)])


def features(x, left):
    def pieces(v):
        first = v.astype(BF16).astype(F32)
        second = (v - first).astype(BF16).astype(F32)
        third = (v - first - second).astype(BF16).astype(F32)
        return first, second, third

    a, b, c = pieces(x)
    norms = pieces(jnp.sum(x * x, 0, keepdims=True))
    ones = (jnp.ones((1, PTS), F32),) * 3
    if left:
        parts = [a, a, b, b, a, c]
        tail = tile_rows(norms + ones)
    else:
        a, b, c = -2.0 * a, -2.0 * b, -2.0 * c
        parts = [a, b, a, b, c, a]
        tail = tile_rows(ones + norms)
    return jnp.concatenate(parts + [tail, jnp.zeros((PTS - 6 * COLS - 8, PTS), F32)], 0)


def slab(i):
    return pl.ds(pl.multiple_of(i * PTS, PTS), PTS)


def matern_block(left, right, high, low, left_f, right_f):
    for j in range(NG):
        at = slice(j * PTS, (j + 1) * PTS)
        right_f[:, at] = features(right[j, 0:COLS] * COORD_SCALE, False).astype(BF16)
        left_f[at, :] = features(left[j, 0:COLS] * COORD_SCALE, True).T.astype(BF16)
    width = 256

    def step(i, carry):
        lhs = left_f[slab(i), :]
        for j in range(0, NG * PTS, width):
            s = jnp.dot(lhs, right_f[:, j : j + width], preferred_element_type=F32)
            s = jnp.maximum(s, 1e-30)
            v = s * lax.rsqrt(s)
            k = ((LN2 * LN2 / 3.0 * s + 1.0) + LN2 * v) * jnp.exp2(-v)
            h = k.astype(BF16)
            high[slab(i), j : j + width] = h
            low[slab(i), j : j + width] = (k - h.astype(F32)).astype(BF16)
        return carry

    lax.fori_loop(0, NG, step, 0)


def matvec(directions, high, low, out):
    v = jnp.concatenate([directions[j] for j in range(NG)], 1)
    v_high = v.astype(BF16)
    both = jnp.concatenate([v_high, (v - v_high.astype(F32)).astype(BF16)], 0)
    width = 512
    for j in range(0, NG * PTS, width):
        r = jnp.dot(both, high[:, j : j + width], preferred_element_type=F32)
        r = r[0:COLS] + r[COLS:] + jnp.dot(v_high, low[:, j : j + width], preferred_element_type=F32)
        for b in range(width // PTS):
            out[j // PTS + b] = r[:, b * PTS : (b + 1) * PTS]


def first_kernel(marks, got_a, got_b, out, high, low, z, table, directions, left_f, right_f):
    now = sum_tiles(got_a, COLS)
    for t in range(NT):
        table[t] = now[t]
    column_directions(marks, now, lambda j: got_a[j, LEAF_PART], got_a, directions)
    z[...] = own_direction(marks, directions)
    matern_block(got_a, got_b, high, low, left_f, right_f)
    matvec(directions, high, low, out)


def image0_kernel(got, z, rhs, basis, leaf, q, leaf_part, send):
    q[...] = tree_sum([got[j] for j in range(NG)]) + NOISE * z[...]
    send[0:COLS, :] = dot_nt(q[...], basis[...])
    send[COLS:, :] = tile_rows([pack([rowdot(rhs[...], z[...]), rowdot(z[...], q[...])])])
    leaf_part[...] = dot_nt(q[...], leaf[...])


def second_kernel(marks, got, got0, table0, rhs, q, high, low, out, z, res, table, table_q, sums, directions):
    now = sum_tiles(got, 0)
    total = tree_sum(now[4:8])
    sums[...] = total[0:8]
    alpha = unpack(total[0:1], 0) / unpack(total[0:1], 1)
    for t in range(NT):
        table_q[t] = now[t]
        now[t] = table0[t] - alpha * now[t]
        table[t] = now[t]
    column_directions(
        marks, now, lambda j: got0[j, LEAF_PART] - alpha * got[j, 2 * COLS : 3 * COLS], got0, directions
    )
    z[...] = own_direction(marks, directions)
    res[...] = rhs[...] - alpha * q[...]
    matvec(directions, high, low, out)


def image1_kernel(got, z1, z0, res, q, leaf, basis, p, send):
    p[...] = tree_sum([got[j] for j in range(NG)]) + NOISE * z1[...]
    send[0:COLS, :] = dot_nt(p[...], basis[...])
    rv, qv, pv, zv = res[...], q[...], p[...], z1[...]
    rb, qb, pb = (dot_nt(v, leaf[...]) for v in (rv, qv, pv))
    rows = [
        pack([rowdot(rv, zv), rowdot(zv, pv), rowdot(zv, qv), rowdot(z0[...], pv)]),
        pack([rowdot(rv, rb), rowdot(rv, qb), rowdot(rv, pb)]),
        pack([rowdot(qv, qb), rowdot(qv, pb), rowdot(pv, pb)]),
    ]
    send[COLS:, :] = tile_rows(rows)


def finish_kernel(got, z0, z1, res, q, p, table1, table_q, sums0, x_out, r_out, coefs):
    now = sum_tiles(got, 0)
    sums = tree_sum(now[4:8])
    rz0, z0q = unpack(sums0[0:1, :], 0), unpack(sums0[0:1, :], 1)
    rz1, z1p, z1q, z0p = (unpack(sums[0:1], k) for k in range(4))
    rbr, rbq, rbp = (unpack(sums[1:2], k) for k in range(3))
    qbq, qbp, pbp = (unpack(sums[2:3], k) for k in range(3))
    alpha0 = rz0 / z0q
    beta0 = rz1 / rz0
    alpha1 = rz1 / (z1p + beta0 * (z1q + z0p) + beta0 * beta0 * z0q)
    image = p[...] + beta0 * q[...]
    r_out[...] = res[...] - alpha1 * image
    x_out[...] = alpha0 * z0[...] + alpha1 * (z1[...] + beta0 * z0[...])
    leaf_part = (
        rbr
        - 2.0 * alpha1 * (rbp + beta0 * rbq)
        + alpha1 * alpha1 * (pbp + 2.0 * beta0 * qbp + beta0 * beta0 * qbq)
    )
    low = lane((COLS, PTS)) < RANK
    now = [table1[t] - alpha1 * (now[t] + beta0 * table_q[t]) for t in range(NT)]
    top = jnp.where(low, tree_sum(now[0:4]), 0.0)
    squares = top * top + tree_sum([jnp.where(low, 0.0, v * v) for v in now])
    beta1 = (leaf_part + jnp.sum(squares, 1, keepdims=True)) / rz1
    for k, v in enumerate((alpha0, alpha1, beta0, beta1)):
        coefs[k // 2, k % 2 : k % 2 + 1, :] = pack([v])[:, 0:COLS]


def gather(block, axes):
    return lax.all_to_all(jnp.broadcast_to(block[None], (NG,) + block.shape), axes, 0, 0, tiled=True)


def scatter(parts):
    return lax.all_to_all(parts, GB, 0, 0, tiled=True)


def on_device(points, inverse_length, target, probe_bits, leaf_inverse, top_basis, sub_basis):
    vec = ((COLS, PTS), F32)
    square = ((PTS, PTS), F32)
    table = ((NT, COLS, PTS), F32)
    block = ((NG * PTS, NG * PTS), BF16)
    parts = ((NG, COLS, PTS), F32)
    wide = ((COLS + 8, PTS), F32)
    dma = pltpu.SemaphoreType.DMA
    where = lax.axis_index(("zl",) + GA).astype(jnp.int32).reshape(1)
    send, rhs, basis, leaf, leaf_part, marks = call(
        start_kernel,
        [((2 * COLS, PTS), F32), vec, square, square, vec, ((NG + 8, PTS), F32)],
        where, inverse_length, points, target[None, :], probe_bits, top_basis, sub_basis, leaf_inverse,
        spaces=[SMEM] + [HBM] * 7,
        scratch=[
            pltpu.VMEM((COLS, PTS), F32), pltpu.VMEM((1, PTS), F32), pltpu.VMEM((COLS - 1, PTS), jnp.int32),
            pltpu.SMEM((COLS,), F32), dma((7,)),
        ],
        name="start",
    )
    got_b = gather(send, GB)
    (send,) = call(fold0_kernel, [((SEND0, PTS), F32)], got_b, send, basis, leaf_part, name="fold0")
    got_a = gather(send, GA)
    out, high, low, z0, table0 = call(
        first_kernel, [parts, block, block, vec, table], marks, got_a, got_b, limit=24 << 20,
        scratch=[
            pltpu.VMEM((NG, COLS, PTS), F32), pltpu.VMEM((NG * PTS, PTS), BF16), pltpu.VMEM((PTS, NG * PTS), BF16)
        ],
        name="first",
    )
    q, leaf_part, send = call(image0_kernel, [vec, vec, wide], scatter(out), z0, rhs, basis, leaf, name="image0")
    (send,) = call(fold1_kernel, [((3 * COLS, PTS), F32)], gather(send, GB), leaf_part, name="fold1")
    out, z1, res, table1, table_q, sums0 = call(
        second_kernel, [parts, vec, vec, table, table, ((8, PTS), F32)],
        marks, gather(send, GA), got_a, table0, rhs, q, high, low,
        limit=24 << 20, scratch=[pltpu.VMEM((NG, COLS, PTS), F32)], name="second",
    )
    p, send = call(image1_kernel, [vec, wide], scatter(out), z1, z0, res, q, leaf, basis, name="image1")
    (send,) = call(fold2_kernel, [((2 * COLS, PTS), F32)], gather(send, GB), name="fold2")
    x_out, r_out, coefs = call(
        finish_kernel, [vec, vec, ((2, 2, COLS), F32)],
        gather(send, GA), z0, z1, res, q, p, table1, table_q, sums0, name="finish",
    )
    return x_out, r_out, coefs


def solution(mesh):
    named = Mesh(mesh.devices.reshape(2, 4, 4, 4, 2), AXES)
    return jax.shard_map(
        on_device,
        mesh=named,
        in_specs=(P(None, AXES), P(), P(AXES), P(None, AXES), P(AXES, None), P(None, AXES), P(None, AXES)),
        out_specs=(P(None, AXES), P(None, AXES), P()),
        check_vma=False,
    )
```

```python
import functools
import math

import jax
import jax.numpy as jnp
from jax import lax
from jax.experimental import pallas as pl
from jax.experimental.pallas import tpu as pltpu
from jax.sharding import Mesh
from jax.sharding import PartitionSpec as P

AXES = ("zl", "y", "zh", "x", "c")
GA = ("y", "x")
GB = ("zl", "zh", "c")
NG = 16
NT = 8
COLS = 16
PTS = 128
RANK = 64
NOISE = 0.5
F32 = jnp.float32
BF16 = jnp.bfloat16
LN2 = math.log(2.0)
COORD_SCALE = math.sqrt(5.0) / LN2
HIGHEST = lax.Precision.HIGHEST


def dot_nt(a, b):
    return lax.dot_general(a, b, (((1,), (1,)), ((), ())), precision=HIGHEST, preferred_element_type=F32)


def dot_nn(a, b):
    return lax.dot_general(a, b, (((1,), (0,)), ((), ())), precision=HIGHEST, preferred_element_type=F32)


def lane(shape):
    return lax.broadcasted_iota(jnp.int32, shape, 1)


def sublane(shape):
    return lax.broadcasted_iota(jnp.int32, shape, 0)


def pack(sums):
    shape = (COLS, PTS)
    acc = jnp.zeros(shape, F32)
    for k, s in enumerate(sums):
        acc = jnp.where(lane(shape) == COLS * k + sublane(shape), jnp.broadcast_to(s, shape), acc)
    return jnp.sum(acc, 0, keepdims=True)


def unpack(row, k):
    shape = (COLS, PTS)
    hit = lane(shape) == COLS * k + sublane(shape)
    return jnp.sum(jnp.where(hit, jnp.broadcast_to(row, shape), 0.0), 1, keepdims=True)


def rowdot(a, b):
    return jnp.sum(a * b, 1, keepdims=True)


def tile_rows(rows):
    shape = (8, PTS)
    out = jnp.zeros(shape, F32)
    for k, r in enumerate(rows):
        out = jnp.where(sublane(shape) == k, jnp.broadcast_to(r, shape), out)
    return out


def tree_sum(terms):
    terms = list(terms)
    while len(terms) > 1:
        terms = [terms[i] + terms[i + 1] if i + 1 < len(terms) else terms[i] for i in range(0, len(terms), 2)]
    return terms[0]


VMEM = pltpu.MemorySpace.VMEM
SMEM = pltpu.MemorySpace.SMEM
HBM = pltpu.MemorySpace.HBM


def call(kernel, outs, *args, spaces=None, out_spaces=None, limit=8 << 20, scratch=(), flags=None, name=None):
    spaces = spaces or [VMEM] * len(args)
    out_spaces = out_spaces or [VMEM] * len(outs)
    args = [pltpu.with_memory_space_constraint(a, m) if m is HBM else a for a, m in zip(args, spaces)]
    return pl.pallas_call(
        kernel,
        out_shape=[m(s, d) if m is HBM else jax.ShapeDtypeStruct(s, d) for m, (s, d) in zip(out_spaces, outs)],
        in_specs=[pl.BlockSpec(memory_space=m) for m in spaces],
        out_specs=[pl.BlockSpec(memory_space=m) for m in out_spaces],
        scratch_shapes=list(scratch),
        compiler_params=pltpu.CompilerParams(vmem_limit_bytes=limit, flags=flags),
        name=name,
    )(*args)


SEND0 = 12 * COLS
BASES = slice(3 * COLS, 3 * COLS + PTS)
LEAF_PART = slice(11 * COLS, 12 * COLS)


def start_kernel(where, inv_h, points_h, target_h, bits_h, top_h, sub_h, leaf_h, send, rhs, basis, leaf, leaf_part, marks, points, target, bits, inv, sems):
    moves = [
        pltpu.make_async_copy(src, dst, sems.at[k])
        for k, (src, dst) in enumerate(
            [
                (bits_h, bits),
                (target_h, target),
                (top_h, basis.at[pl.ds(0, RANK)]),
                (sub_h, basis.at[pl.ds(RANK, RANK)]),
                (points_h, points),
                (inv_h, inv),
                (leaf_h, leaf),
            ]
        )
    ]
    for m in moves:
        m.start()
    row = sublane((NG + 8, PTS))
    place = where[0]
    hit = (row == lax.rem(place, NG)) | ((row >= NG) & (place >= NG))
    marks[...] = jnp.where(hit, 1.0, 0.0)
    for m in moves:
        m.wait()
    scale = jnp.zeros((COLS, PTS), F32)
    for k in range(COLS):
        scale = jnp.where(sublane((COLS, PTS)) == k, inv[k], scale)
    rhs[0:1, :] = target[...]
    rhs[1:COLS, :] = 2.0 * bits[...].astype(F32) - 1.0
    send[0:COLS, :] = points[...] * scale
    send[COLS : 2 * COLS, :] = dot_nt(rhs[...], basis[...])
    leaf_part[...] = dot_nt(rhs[...], leaf[...])


def fold_tiles(got, first, scalars, send, at):
    low = lane((COLS, PTS)) < RANK
    zero = tree_sum([got[j, first : first + COLS] for j in range(NG // 2)])
    one = tree_sum([got[j, first : first + COLS] for j in range(NG // 2, NG)])
    send[at : at + COLS, :] = jnp.where(low, zero + one, zero)
    send[at + COLS : at + 2 * COLS, :] = jnp.where(low, 0.0, one)
    if scalars:
        own = tree_sum([got[j, scalars : scalars + 8] for j in range(NG)])
        send[at + COLS : at + COLS + 8, :] = jnp.where(low[0:8], own, one[0:8])


def fold0_kernel(got, own, basis, leaf_part, send):
    send[0:COLS, :] = own[0:COLS, :]
    fold_tiles(got, COLS, 0, send, COLS)
    send[BASES, :] = basis[...]
    send[LEAF_PART, :] = leaf_part[...]


def fold1_kernel(got, leaf_part, send):
    fold_tiles(got, 0, COLS, send, 0)
    send[2 * COLS : 3 * COLS, :] = leaf_part[...]


def fold2_kernel(got, send):
    fold_tiles(got, 0, COLS, send, 0)


def sum_tiles(got, first):
    return [
        tree_sum([got[4 * y + x, at : at + COLS] for x in range(4)]) for at in (first, first + COLS) for y in range(4)
    ]


def column_directions(marks, table, leaf_parts, got0, directions):
    low = lane((COLS, PTS)) < RANK
    odd = marks[NG : NG + 1, :] > 0.5
    top = tree_sum(table[0:4])
    for y in range(4):
        coefs = jnp.where(low, top, jnp.where(odd, table[4 + y], table[y]))
        high = coefs.astype(BF16)
        both = jnp.concatenate([high, (coefs - high.astype(F32)).astype(BF16)], 0)
        for j in range(4 * y, 4 * y + 4):
            bases = got0[j, BASES]
            first = bases.astype(BF16)
            r = jnp.dot(both, first, preferred_element_type=F32)
            r = r[0:COLS] + r[COLS:] + jnp.dot(high, (bases - first.astype(F32)).astype(BF16), preferred_element_type=F32)
            directions[j] = leaf_parts(j) + r


def own_direction(marks, directions):
    return tree_sum([directions[j] * marks[j : j + 1, :] for j in range(NG)])


def features(x, left):
    def pieces(v):
        first = v.astype(BF16).astype(F32)
        second = (v - first).astype(BF16).astype(F32)
        third = (v - first - second).astype(BF16).astype(F32)
        return first, second, third

    a, b, c = pieces(x)
    norms = pieces(jnp.sum(x * x, 0, keepdims=True))
    ones = (jnp.ones((1, PTS), F32),) * 3
    if left:
        parts = [a, a, b, b, a, c]
        tail = tile_rows(norms + ones)
    else:
        a, b, c = -2.0 * a, -2.0 * b, -2.0 * c
        parts = [a, b, a, b, c, a]
        tail = tile_rows(ones + norms)
    return jnp.concatenate(parts + [tail, jnp.zeros((PTS - 6 * COLS - 8, PTS), F32)], 0)


def matern_kernel(left, right, high, low, left_f, right_f):
    for j in range(NG):
        at = slice(j * PTS, (j + 1) * PTS)
        right_f[:, at] = features(right[j, 0:COLS] * COORD_SCALE, False).astype(BF16)
        left_f[at, :] = features(left[j, 0:COLS] * COORD_SCALE, True).T.astype(BF16)
    height, width = 1024, 256

    def step(i, carry):
        rows = pl.ds(pl.multiple_of(i * height, height), height)
        lhs = left_f[rows, :]
        for j in range(0, NG * PTS, width):
            s = jnp.dot(lhs, right_f[:, j : j + width], preferred_element_type=F32)
            s = jnp.maximum(s, 1e-30)
            v = s * lax.rsqrt(s)
            k = ((LN2 * LN2 / 3.0 * v + LN2) * v + 1.0) * jnp.exp2(-v)
            h = k.astype(BF16)
            high[rows, j : j + width] = h
            low[rows, j : j + width] = (k - h.astype(F32)).astype(BF16)
        return carry

    lax.fori_loop(0, NG * PTS // height, step, 0)


def matvec(directions, high, low, out):
    v = jnp.concatenate([directions[j] for j in range(NG)], 1)
    v_high = v.astype(BF16)
    both = jnp.concatenate([v_high, (v - v_high.astype(F32)).astype(BF16)], 0)
    width = 512
    for j in range(0, NG * PTS, width):
        r = jnp.dot(both, high[:, j : j + width], preferred_element_type=F32)
        r = r[0:COLS] + r[COLS:] + jnp.dot(v_high, low[:, j : j + width], preferred_element_type=F32)
        for b in range(width // PTS):
            out[j // PTS + b] = r[:, b * PTS : (b + 1) * PTS]


def first_kernel(marks, got_a, high, low, out, z, table, directions):
    now = sum_tiles(got_a, COLS)
    for t in range(NT):
        table[t] = now[t]
    column_directions(marks, now, lambda j: got_a[j, LEAF_PART], got_a, directions)
    z[...] = own_direction(marks, directions)
    matvec(directions, high, low, out)


def image0_kernel(got, z, rhs, basis, leaf, q, leaf_part, send):
    q[...] = tree_sum([got[j] for j in range(NG)]) + NOISE * z[...]
    send[0:COLS, :] = dot_nt(q[...], basis[...])
    send[COLS:, :] = tile_rows([pack([rowdot(rhs[...], z[...]), rowdot(z[...], q[...])])])
    leaf_part[...] = dot_nt(q[...], leaf[...])


def second_kernel(marks, got, got0, table0, rhs, q, high, low, out, z, res, table, table_q, sums, directions):
    now = sum_tiles(got, 0)
    total = tree_sum(now[4:8])
    sums[...] = total[0:8]
    alpha = unpack(total[0:1], 0) / unpack(total[0:1], 1)
    for t in range(NT):
        table_q[t] = now[t]
        now[t] = table0[t] - alpha * now[t]
        table[t] = now[t]
    column_directions(
        marks, now, lambda j: got0[j, LEAF_PART] - alpha * got[j, 2 * COLS : 3 * COLS], got0, directions
    )
    z[...] = own_direction(marks, directions)
    res[...] = rhs[...] - alpha * q[...]
    matvec(directions, high, low, out)


def image1_kernel(got, z1, z0, res, q, leaf, basis, p, send):
    p[...] = tree_sum([got[j] for j in range(NG)]) + NOISE * z1[...]
    send[0:COLS, :] = dot_nt(p[...], basis[...])
    rv, qv, pv, zv = res[...], q[...], p[...], z1[...]
    rb, qb, pb = (dot_nt(v, leaf[...]) for v in (rv, qv, pv))
    rows = [
        pack([rowdot(rv, zv), rowdot(zv, pv), rowdot(zv, qv), rowdot(z0[...], pv)]),
        pack([rowdot(rv, rb), rowdot(rv, qb), rowdot(rv, pb)]),
        pack([rowdot(qv, qb), rowdot(qv, pb), rowdot(pv, pb)]),
    ]
    send[COLS:, :] = tile_rows(rows)


def finish_kernel(got, z0, z1, res, q, p, table1, table_q, sums0, x_out, r_out, coefs):
    now = sum_tiles(got, 0)
    sums = tree_sum(now[4:8])
    rz0, z0q = unpack(sums0[0:1, :], 0), unpack(sums0[0:1, :], 1)
    rz1, z1p, z1q, z0p = (unpack(sums[0:1], k) for k in range(4))
    rbr, rbq, rbp = (unpack(sums[1:2], k) for k in range(3))
    qbq, qbp, pbp = (unpack(sums[2:3], k) for k in range(3))
    alpha0 = rz0 / z0q
    beta0 = rz1 / rz0
    alpha1 = rz1 / (z1p + beta0 * (z1q + z0p) + beta0 * beta0 * z0q)
    image = p[...] + beta0 * q[...]
    r_out[...] = res[...] - alpha1 * image
    x_out[...] = alpha0 * z0[...] + alpha1 * (z1[...] + beta0 * z0[...])
    leaf_part = (
        rbr
        - 2.0 * alpha1 * (rbp + beta0 * rbq)
        + alpha1 * alpha1 * (pbp + 2.0 * beta0 * qbp + beta0 * beta0 * qbq)
    )
    low = lane((COLS, PTS)) < RANK
    now = [table1[t] - alpha1 * (now[t] + beta0 * table_q[t]) for t in range(NT)]
    top = jnp.where(low, tree_sum(now[0:4]), 0.0)
    squares = top * top + tree_sum([jnp.where(low, 0.0, v * v) for v in now])
    beta1 = (leaf_part + jnp.sum(squares, 1, keepdims=True)) / rz1
    for k, v in enumerate((alpha0, alpha1, beta0, beta1)):
        coefs[k // 2, k % 2 : k % 2 + 1, :] = pack([v])[:, 0:COLS]


def gather(block, axes):
    return lax.all_to_all(jnp.broadcast_to(block[None], (NG,) + block.shape), axes, 0, 0, tiled=True)


def scatter(parts):
    return lax.all_to_all(parts, GB, 0, 0, tiled=True)


def on_device(points, inverse_length, target, probe_bits, leaf_inverse, top_basis, sub_basis):
    vec = ((COLS, PTS), F32)
    square = ((PTS, PTS), F32)
    table = ((NT, COLS, PTS), F32)
    block = ((NG * PTS, NG * PTS), BF16)
    parts = ((NG, COLS, PTS), F32)
    wide = ((COLS + 8, PTS), F32)
    dma = pltpu.SemaphoreType.DMA
    where = lax.axis_index(("zl",) + GA).astype(jnp.int32).reshape(1)
    send, rhs, basis, leaf, leaf_part, marks = call(
        start_kernel,
        [((2 * COLS, PTS), F32), vec, square, square, vec, ((NG + 8, PTS), F32)],
        where, inverse_length, points, target[None, :], probe_bits, top_basis, sub_basis, leaf_inverse,
        spaces=[SMEM] + [HBM] * 7,
        scratch=[
            pltpu.VMEM((COLS, PTS), F32), pltpu.VMEM((1, PTS), F32), pltpu.VMEM((COLS - 1, PTS), jnp.int32),
            pltpu.SMEM((COLS,), F32), dma((7,)),
        ],
        name="start",
    )
    got_b = gather(send, GB)
    (send,) = call(fold0_kernel, [((SEND0, PTS), F32)], got_b, send, basis, leaf_part, name="fold0")
    got_a = gather(send, GA)
    high, low = call(
        matern_kernel, [block, block], got_a, got_b, limit=24 << 20,
        scratch=[pltpu.VMEM((NG * PTS, PTS), BF16), pltpu.VMEM((PTS, NG * PTS), BF16)],
        name="matern",
    )
    out, z0, table0 = call(
        first_kernel, [parts, vec, table], marks, got_a, high, low,
        limit=24 << 20, scratch=[pltpu.VMEM((NG, COLS, PTS), F32)], name="first",
    )
    q, leaf_part, send = call(image0_kernel, [vec, vec, wide], scatter(out), z0, rhs, basis, leaf, name="image0")
    (send,) = call(fold1_kernel, [((3 * COLS, PTS), F32)], gather(send, GB), leaf_part, name="fold1")
    out, z1, res, table1, table_q, sums0 = call(
        second_kernel, [parts, vec, vec, table, table, ((8, PTS), F32)],
        marks, gather(send, GA), got_a, table0, rhs, q, high, low,
        limit=24 << 20, scratch=[pltpu.VMEM((NG, COLS, PTS), F32)], name="second",
    )
    p, send = call(image1_kernel, [vec, wide], scatter(out), z1, z0, res, q, leaf, basis, name="image1")
    (send,) = call(fold2_kernel, [((2 * COLS, PTS), F32)], gather(send, GB), name="fold2")
    x_out, r_out, coefs = call(
        finish_kernel, [vec, vec, ((2, 2, COLS), F32)],
        gather(send, GA), z0, z1, res, q, p, table1, table_q, sums0, name="finish",
    )
    return x_out, r_out, coefs


def solution(mesh):
    named = Mesh(mesh.devices.reshape(2, 4, 4, 4, 2), AXES)
    return jax.shard_map(
        on_device,
        mesh=named,
        in_specs=(P(None, AXES), P(), P(AXES), P(None, AXES), P(AXES, None), P(None, AXES), P(None, AXES)),
        out_specs=(P(None, AXES), P(None, AXES), P()),
        check_vma=False,
    )
```

```python
import functools
import math

import jax
import jax.numpy as jnp
from jax import lax
from jax.experimental import pallas as pl
from jax.experimental.pallas import tpu as pltpu
from jax.sharding import Mesh
from jax.sharding import PartitionSpec as P

AXES = ("zl", "y", "zh", "x", "c")
GA = ("y", "x")
GB = ("zl", "zh", "c")
NG = 16
NT = 8
COLS = 16
PTS = 128
RANK = 64
NOISE = 0.5
F32 = jnp.float32
BF16 = jnp.bfloat16
LN2 = math.log(2.0)
COORD_SCALE = math.sqrt(5.0) / LN2
LEAD = LN2 * LN2 / 3.0
SHIFT = 1.5 / LN2
REST = 1.0 / LEAD - SHIFT * SHIFT
HIGHEST = lax.Precision.HIGHEST


def dot_nt(a, b):
    return lax.dot_general(a, b, (((1,), (1,)), ((), ())), precision=HIGHEST, preferred_element_type=F32)


def dot_nn(a, b):
    return lax.dot_general(a, b, (((1,), (0,)), ((), ())), precision=HIGHEST, preferred_element_type=F32)


def lane(shape):
    return lax.broadcasted_iota(jnp.int32, shape, 1)


def sublane(shape):
    return lax.broadcasted_iota(jnp.int32, shape, 0)


def pack(sums):
    shape = (COLS, PTS)
    acc = jnp.zeros(shape, F32)
    for k, s in enumerate(sums):
        acc = jnp.where(lane(shape) == COLS * k + sublane(shape), jnp.broadcast_to(s, shape), acc)
    return jnp.sum(acc, 0, keepdims=True)


def unpack(row, k):
    shape = (COLS, PTS)
    hit = lane(shape) == COLS * k + sublane(shape)
    return jnp.sum(jnp.where(hit, jnp.broadcast_to(row, shape), 0.0), 1, keepdims=True)


def rowdot(a, b):
    return jnp.sum(a * b, 1, keepdims=True)


def tile_rows(rows):
    shape = (8, PTS)
    out = jnp.zeros(shape, F32)
    for k, r in enumerate(rows):
        out = jnp.where(sublane(shape) == k, jnp.broadcast_to(r, shape), out)
    return out


def tree_sum(terms):
    terms = list(terms)
    while len(terms) > 1:
        terms = [terms[i] + terms[i + 1] if i + 1 < len(terms) else terms[i] for i in range(0, len(terms), 2)]
    return terms[0]


VMEM = pltpu.MemorySpace.VMEM
SMEM = pltpu.MemorySpace.SMEM
HBM = pltpu.MemorySpace.HBM


def call(kernel, outs, *args, spaces=None, out_spaces=None, limit=8 << 20, scratch=(), name=None):
    spaces = spaces or [VMEM] * len(args)
    out_spaces = out_spaces or [VMEM] * len(outs)
    args = [pltpu.with_memory_space_constraint(a, m) if m is HBM else a for a, m in zip(args, spaces)]
    return pl.pallas_call(
        kernel,
        out_shape=[m(s, d) if m is HBM else jax.ShapeDtypeStruct(s, d) for m, (s, d) in zip(out_spaces, outs)],
        in_specs=[pl.BlockSpec(memory_space=m) for m in spaces],
        out_specs=[pl.BlockSpec(memory_space=m) for m in out_spaces],
        scratch_shapes=list(scratch),
        compiler_params=pltpu.CompilerParams(vmem_limit_bytes=limit),
        name=name,
    )(*args)


SEND0 = 12 * COLS
BASES = slice(3 * COLS, 3 * COLS + PTS)
LEAF_PART = slice(11 * COLS, 12 * COLS)


def start_kernel(where, inv_h, points_h, target_h, bits_h, top_h, sub_h, leaf_h, send, rhs, basis, leaf, leaf_part, marks, points, target, bits, inv, sems):
    moves = [
        pltpu.make_async_copy(src, dst, sems.at[k])
        for k, (src, dst) in enumerate(
            [
                (bits_h, bits),
                (target_h, target),
                (top_h, basis.at[pl.ds(0, RANK)]),
                (sub_h, basis.at[pl.ds(RANK, RANK)]),
                (points_h, points),
                (inv_h, inv),
                (leaf_h, leaf),
            ]
        )
    ]
    for m in moves:
        m.start()
    row = sublane((NG + 8, PTS))
    place = where[0]
    hit = (row == lax.rem(place, NG)) | ((row >= NG) & (place >= NG))
    marks[...] = jnp.where(hit, 1.0, 0.0)
    for m in moves:
        m.wait()
    scale = jnp.zeros((COLS, PTS), F32)
    for k in range(COLS):
        scale = jnp.where(sublane((COLS, PTS)) == k, inv[k], scale)
    rhs[0:1, :] = target[...]
    rhs[1:COLS, :] = 2.0 * bits[...].astype(F32) - 1.0
    send[0:COLS, :] = points[...] * scale
    send[COLS : 2 * COLS, :] = dot_nt(rhs[...], basis[...])
    leaf_part[...] = dot_nt(rhs[...], leaf[...])


def fold_tiles(got, first, scalars, send, at):
    low = lane((COLS, PTS)) < RANK
    zero = tree_sum([got[j, first : first + COLS] for j in range(NG // 2)])
    one = tree_sum([got[j, first : first + COLS] for j in range(NG // 2, NG)])
    send[at : at + COLS, :] = jnp.where(low, zero + one, zero)
    send[at + COLS : at + 2 * COLS, :] = jnp.where(low, 0.0, one)
    if scalars:
        own = tree_sum([got[j, scalars : scalars + 8] for j in range(NG)])
        send[at + COLS : at + COLS + 8, :] = jnp.where(low[0:8], own, one[0:8])


def fold0_kernel(got, own, basis, leaf_part, send):
    send[0:COLS, :] = own[0:COLS, :]
    fold_tiles(got, COLS, 0, send, COLS)
    send[BASES, :] = basis[...]
    send[LEAF_PART, :] = leaf_part[...]


def fold1_kernel(got, leaf_part, send):
    fold_tiles(got, 0, COLS, send, 0)
    send[2 * COLS : 3 * COLS, :] = leaf_part[...]


def fold2_kernel(got, send):
    fold_tiles(got, 0, COLS, send, 0)


def sum_tiles(got, first):
    return [
        tree_sum([got[4 * y + x, at : at + COLS] for x in range(4)]) for at in (first, first + COLS) for y in range(4)
    ]


def column_directions(marks, table, leaf_parts, got0, directions):
    low = lane((COLS, PTS)) < RANK
    odd = marks[NG : NG + 1, :] > 0.5
    top = tree_sum(table[0:4])
    for y in range(4):
        coefs = jnp.where(low, top, jnp.where(odd, table[4 + y], table[y]))
        high = coefs.astype(BF16)
        both = jnp.concatenate([high, (coefs - high.astype(F32)).astype(BF16)], 0)
        for j in range(4 * y, 4 * y + 4):
            bases = got0[j, BASES]
            first = bases.astype(BF16)
            r = jnp.dot(both, first, preferred_element_type=F32)
            r = r[0:COLS] + r[COLS:] + jnp.dot(high, (bases - first.astype(F32)).astype(BF16), preferred_element_type=F32)
            directions[j] = leaf_parts(j) + r


def own_direction(marks, directions):
    return tree_sum([directions[j] * marks[j : j + 1, :] for j in range(NG)])


def features(x, left):
    def pieces(v):
        first = v.astype(BF16).astype(F32)
        second = (v - first).astype(BF16).astype(F32)
        third = (v - first - second).astype(BF16).astype(F32)
        return first, second, third

    a, b, c = pieces(x)
    norms = pieces(jnp.sum(x * x, 0, keepdims=True))
    ones = (jnp.ones((1, PTS), F32),) * 3
    if left:
        parts = [a, a, b, b, a, c]
        tail = tile_rows(norms + ones)
    else:
        a, b, c = -2.0 * a, -2.0 * b, -2.0 * c
        parts = [a, b, a, b, c, a]
        tail = tile_rows(ones + norms)
    return jnp.concatenate(parts + [tail, jnp.zeros((PTS - 6 * COLS - 8, PTS), F32)], 0)


def matern_kernel(left, right, high, low, left_f, right_f):
    for j in range(NG):
        at = slice(j * PTS, (j + 1) * PTS)
        right_f[:, at] = features(right[j, 0:COLS] * COORD_SCALE, False).astype(BF16)
        left_f[at, :] = features(left[j, 0:COLS] * COORD_SCALE, True).T.astype(BF16)
    height, width = 1024, 256

    def step(i, carry):
        rows = pl.ds(pl.multiple_of(i * height, height), height)
        lhs = left_f[rows, :]
        for j in range(0, NG * PTS, width):
            s = jnp.dot(lhs, right_f[:, j : j + width], preferred_element_type=F32)
            s = jnp.maximum(s, 1e-30)
            v = s * lax.rsqrt(s)
            w = v + SHIFT
            k = (w * w + REST) * jnp.exp2(-v)
            h = k.astype(BF16)
            high[rows, j : j + width] = h
            low[rows, j : j + width] = (k - h.astype(F32)).astype(BF16)
        return carry

    lax.fori_loop(0, NG * PTS // height, step, 0)


def matvec(directions, high, low, out):
    v = jnp.concatenate([directions[j] * LEAD for j in range(NG)], 1)
    v_high = v.astype(BF16)
    both = jnp.concatenate([v_high, (v - v_high.astype(F32)).astype(BF16)], 0)
    width = 512
    for j in range(0, NG * PTS, width):
        r = jnp.dot(both, high[:, j : j + width], preferred_element_type=F32)
        r = r[0:COLS] + r[COLS:] + jnp.dot(v_high, low[:, j : j + width], preferred_element_type=F32)
        for b in range(width // PTS):
            out[j // PTS + b] = r[:, b * PTS : (b + 1) * PTS]


def first_kernel(marks, got_a, high, low, out, z, table, directions):
    now = sum_tiles(got_a, COLS)
    for t in range(NT):
        table[t] = now[t]
    column_directions(marks, now, lambda j: got_a[j, LEAF_PART], got_a, directions)
    z[...] = own_direction(marks, directions)
    matvec(directions, high, low, out)


def image0_kernel(got, z, rhs, basis, leaf, q, leaf_part, send):
    q[...] = tree_sum([got[j] for j in range(NG)]) + NOISE * z[...]
    send[0:COLS, :] = dot_nt(q[...], basis[...])
    send[COLS:, :] = tile_rows([pack([rowdot(rhs[...], z[...]), rowdot(z[...], q[...])])])
    leaf_part[...] = dot_nt(q[...], leaf[...])


def second_kernel(marks, got, got0, table0, rhs, q, high, low, out, z, res, table, table_q, sums, directions):
    now = sum_tiles(got, 0)
    total = tree_sum(now[4:8])
    sums[...] = total[0:8]
    alpha = unpack(total[0:1], 0) / unpack(total[0:1], 1)
    for t in range(NT):
        table_q[t] = now[t]
        now[t] = table0[t] - alpha * now[t]
        table[t] = now[t]
    column_directions(
        marks, now, lambda j: got0[j, LEAF_PART] - alpha * got[j, 2 * COLS : 3 * COLS], got0, directions
    )
    z[...] = own_direction(marks, directions)
    res[...] = rhs[...] - alpha * q[...]
    matvec(directions, high, low, out)


def image1_kernel(got, z1, z0, res, q, leaf, basis, p, send):
    p[...] = tree_sum([got[j] for j in range(NG)]) + NOISE * z1[...]
    send[0:COLS, :] = dot_nt(p[...], basis[...])
    rv, qv, pv, zv = res[...], q[...], p[...], z1[...]
    rb, qb, pb = (dot_nt(v, leaf[...]) for v in (rv, qv, pv))
    rows = [
        pack([rowdot(rv, zv), rowdot(zv, pv), rowdot(zv, qv), rowdot(z0[...], pv)]),
        pack([rowdot(rv, rb), rowdot(rv, qb), rowdot(rv, pb)]),
        pack([rowdot(qv, qb), rowdot(qv, pb), rowdot(pv, pb)]),
    ]
    send[COLS:, :] = tile_rows(rows)


def finish_kernel(got, z0, z1, res, q, p, table1, table_q, sums0, x_out, r_out, coefs):
    now = sum_tiles(got, 0)
    sums = tree_sum(now[4:8])
    rz0, z0q = unpack(sums0[0:1, :], 0), unpack(sums0[0:1, :], 1)
    rz1, z1p, z1q, z0p = (unpack(sums[0:1], k) for k in range(4))
    rbr, rbq, rbp = (unpack(sums[1:2], k) for k in range(3))
    qbq, qbp, pbp = (unpack(sums[2:3], k) for k in range(3))
    alpha0 = rz0 / z0q
    beta0 = rz1 / rz0
    alpha1 = rz1 / (z1p + beta0 * (z1q + z0p) + beta0 * beta0 * z0q)
    image = p[...] + beta0 * q[...]
    r_out[...] = res[...] - alpha1 * image
    x_out[...] = alpha0 * z0[...] + alpha1 * (z1[...] + beta0 * z0[...])
    leaf_part = (
        rbr
        - 2.0 * alpha1 * (rbp + beta0 * rbq)
        + alpha1 * alpha1 * (pbp + 2.0 * beta0 * qbp + beta0 * beta0 * qbq)
    )
    low = lane((COLS, PTS)) < RANK
    now = [table1[t] - alpha1 * (now[t] + beta0 * table_q[t]) for t in range(NT)]
    top = jnp.where(low, tree_sum(now[0:4]), 0.0)
    squares = top * top + tree_sum([jnp.where(low, 0.0, v * v) for v in now])
    beta1 = (leaf_part + jnp.sum(squares, 1, keepdims=True)) / rz1
    for k, v in enumerate((alpha0, alpha1, beta0, beta1)):
        coefs[k // 2, k % 2 : k % 2 + 1, :] = pack([v])[:, 0:COLS]


def gather(block, axes):
    return lax.all_to_all(jnp.broadcast_to(block[None], (NG,) + block.shape), axes, 0, 0, tiled=True)


def scatter(parts):
    return lax.all_to_all(parts, GB, 0, 0, tiled=True)


def on_device(points, inverse_length, target, probe_bits, leaf_inverse, top_basis, sub_basis):
    vec = ((COLS, PTS), F32)
    square = ((PTS, PTS), F32)
    table = ((NT, COLS, PTS), F32)
    block = ((NG * PTS, NG * PTS), BF16)
    parts = ((NG, COLS, PTS), F32)
    wide = ((COLS + 8, PTS), F32)
    dma = pltpu.SemaphoreType.DMA
    where = lax.axis_index(("zl",) + GA).astype(jnp.int32).reshape(1)
    send, rhs, basis, leaf, leaf_part, marks = call(
        start_kernel,
        [((2 * COLS, PTS), F32), vec, square, square, vec, ((NG + 8, PTS), F32)],
        where, inverse_length, points, target[None, :], probe_bits, top_basis, sub_basis, leaf_inverse,
        spaces=[SMEM] + [HBM] * 7,
        scratch=[
            pltpu.VMEM((COLS, PTS), F32), pltpu.VMEM((1, PTS), F32), pltpu.VMEM((COLS - 1, PTS), jnp.int32),
            pltpu.SMEM((COLS,), F32), dma((7,)),
        ],
        name="start",
    )
    got_b = gather(send, GB)
    (send,) = call(fold0_kernel, [((SEND0, PTS), F32)], got_b, send, basis, leaf_part, name="fold0")
    got_a = gather(send, GA)
    high, low = call(
        matern_kernel, [block, block], got_a, got_b, limit=24 << 20,
        scratch=[pltpu.VMEM((NG * PTS, PTS), BF16), pltpu.VMEM((PTS, NG * PTS), BF16)],
        name="matern",
    )
    out, z0, table0 = call(
        first_kernel, [parts, vec, table], marks, got_a, high, low,
        limit=24 << 20, scratch=[pltpu.VMEM((NG, COLS, PTS), F32)], name="first",
    )
    q, leaf_part, send = call(image0_kernel, [vec, vec, wide], scatter(out), z0, rhs, basis, leaf, name="image0")
    (send,) = call(fold1_kernel, [((3 * COLS, PTS), F32)], gather(send, GB), leaf_part, name="fold1")
    out, z1, res, table1, table_q, sums0 = call(
        second_kernel, [parts, vec, vec, table, table, ((8, PTS), F32)],
        marks, gather(send, GA), got_a, table0, rhs, q, high, low,
        limit=24 << 20, scratch=[pltpu.VMEM((NG, COLS, PTS), F32)], name="second",
    )
    p, send = call(image1_kernel, [vec, wide], scatter(out), z1, z0, res, q, leaf, basis, name="image1")
    (send,) = call(fold2_kernel, [((2 * COLS, PTS), F32)], gather(send, GB), name="fold2")
    x_out, r_out, coefs = call(
        finish_kernel, [vec, vec, ((2, 2, COLS), F32)],
        gather(send, GA), z0, z1, res, q, p, table1, table_q, sums0, name="finish",
    )
    return x_out, r_out, coefs


def solution(mesh):
    named = Mesh(mesh.devices.reshape(2, 4, 4, 4, 2), AXES)
    return jax.shard_map(
        on_device,
        mesh=named,
        in_specs=(P(None, AXES), P(), P(AXES), P(None, AXES), P(AXES, None), P(None, AXES), P(None, AXES)),
        out_specs=(P(None, AXES), P(None, AXES), P()),
        check_vma=False,
    )
```

```python
import functools
import math

import jax
import jax.numpy as jnp
from jax import lax
from jax.experimental import pallas as pl
from jax.experimental.pallas import tpu as pltpu
from jax.sharding import Mesh
from jax.sharding import PartitionSpec as P

AXES = ("zl", "y", "zh", "x", "c")
GA = ("y", "x")
GB = ("zl", "zh", "c")
NG = 16
NT = 8
COLS = 16
PTS = 128
RANK = 64
NOISE = 0.5
F32 = jnp.float32
BF16 = jnp.bfloat16
LN2 = math.log(2.0)
COORD_SCALE = math.sqrt(5.0) / LN2
LEAD = LN2 * LN2 / 3.0
SHIFT = 1.5 / LN2
REST = 1.0 / LEAD - SHIFT * SHIFT
HIGHEST = lax.Precision.HIGHEST


def dot_nt(a, b):
    return lax.dot_general(a, b, (((1,), (1,)), ((), ())), precision=HIGHEST, preferred_element_type=F32)


def dot_nn(a, b):
    return lax.dot_general(a, b, (((1,), (0,)), ((), ())), precision=HIGHEST, preferred_element_type=F32)


def lane(shape):
    return lax.broadcasted_iota(jnp.int32, shape, 1)


def sublane(shape):
    return lax.broadcasted_iota(jnp.int32, shape, 0)


def pack(sums):
    shape = (COLS, PTS)
    acc = jnp.zeros(shape, F32)
    for k, s in enumerate(sums):
        acc = jnp.where(lane(shape) == COLS * k + sublane(shape), jnp.broadcast_to(s, shape), acc)
    return jnp.sum(acc, 0, keepdims=True)


def unpack(row, k):
    shape = (COLS, PTS)
    hit = lane(shape) == COLS * k + sublane(shape)
    return jnp.sum(jnp.where(hit, jnp.broadcast_to(row, shape), 0.0), 1, keepdims=True)


def rowdot(a, b):
    return jnp.sum(a * b, 1, keepdims=True)


def tile_rows(rows):
    shape = (8, PTS)
    out = jnp.zeros(shape, F32)
    for k, r in enumerate(rows):
        out = jnp.where(sublane(shape) == k, jnp.broadcast_to(r, shape), out)
    return out


def tree_sum(terms):
    terms = list(terms)
    while len(terms) > 1:
        terms = [terms[i] + terms[i + 1] if i + 1 < len(terms) else terms[i] for i in range(0, len(terms), 2)]
    return terms[0]


VMEM = pltpu.MemorySpace.VMEM
SMEM = pltpu.MemorySpace.SMEM
HBM = pltpu.MemorySpace.HBM


def call(kernel, outs, *args, spaces=None, out_spaces=None, limit=8 << 20, scratch=(), name=None):
    spaces = spaces or [VMEM] * len(args)
    out_spaces = out_spaces or [VMEM] * len(outs)
    args = [pltpu.with_memory_space_constraint(a, m) if m is HBM else a for a, m in zip(args, spaces)]
    return pl.pallas_call(
        kernel,
        out_shape=[m(s, d) if m is HBM else jax.ShapeDtypeStruct(s, d) for m, (s, d) in zip(out_spaces, outs)],
        in_specs=[pl.BlockSpec(memory_space=m) for m in spaces],
        out_specs=[pl.BlockSpec(memory_space=m) for m in out_spaces],
        scratch_shapes=list(scratch),
        compiler_params=pltpu.CompilerParams(vmem_limit_bytes=limit),
        name=name,
    )(*args)


SEND0 = 5 * COLS // 2 + PTS + COLS
BASES = slice(5 * COLS // 2, 5 * COLS // 2 + PTS)
LEAF_PART = slice(SEND0 - COLS, SEND0)


def start_kernel(where, inv_h, points_h, target_h, bits_h, top_h, sub_h, leaf_h, send, rhs, basis, leaf, leaf_part, marks, points, target, bits, inv, sems):
    moves = [
        pltpu.make_async_copy(src, dst, sems.at[k])
        for k, (src, dst) in enumerate(
            [
                (bits_h, bits),
                (target_h, target),
                (top_h, basis.at[pl.ds(0, RANK)]),
                (sub_h, basis.at[pl.ds(RANK, RANK)]),
                (points_h, points),
                (inv_h, inv),
                (leaf_h, leaf),
            ]
        )
    ]
    for m in moves:
        m.start()
    row = sublane((NG + 8, PTS))
    place = where[0]
    hit = (row == lax.rem(place, NG)) | ((row >= NG) & (place >= NG))
    marks[...] = jnp.where(hit, 1.0, 0.0)
    for m in moves:
        m.wait()
    scale = jnp.zeros((COLS, PTS), F32)
    for k in range(COLS):
        scale = jnp.where(sublane((COLS, PTS)) == k, inv[k], scale)
    rhs[0:1, :] = target[...]
    rhs[1:COLS, :] = 2.0 * bits[...].astype(F32) - 1.0
    send[0:COLS, :] = points[...] * scale
    send[COLS : 2 * COLS, :] = dot_nt(rhs[...], basis[...])
    leaf_part[...] = dot_nt(rhs[...], leaf[...])


def pack_half(tile):
    return jnp.where(lane((8, PTS)) < RANK, pltpu.roll(tile[0:8], RANK, 1), tile[8:16])


def unpack_half(packed):
    return jnp.concatenate([pltpu.roll(packed, RANK, 1), packed], 0)


def fold0_kernel(got, own, basis, leaf_part, send):
    low = lane((COLS, PTS)) < RANK
    zero = tree_sum([got[j, COLS : 2 * COLS] for j in range(NG // 2)])
    one = tree_sum([got[j, COLS : 2 * COLS] for j in range(NG // 2, NG)])
    send[0:COLS, :] = own[0:COLS, :]
    send[COLS : 2 * COLS, :] = jnp.where(low, zero + one, zero)
    send[2 * COLS : 5 * COLS // 2, :] = pack_half(one)
    send[BASES, :] = basis[...]
    send[LEAF_PART, :] = leaf_part[...]


def fold_rows(got, rows, send, zero, one):
    for r in range(COLS):
        zero[r : r + 1, :] = tree_sum([got[j, r] for j in range(NG // 2)])
        one[r : r + 1, :] = tree_sum([got[j, r] for j in range(NG // 2, NG)])
    own = tile_rows([tree_sum([got[j, r] for j in range(NG)]) for r in range(COLS, rows)])
    low = lane((COLS, PTS)) < RANK
    send[0:COLS, :] = jnp.where(low, zero[...] + one[...], zero[...])
    send[COLS : 2 * COLS, :] = jnp.where(low, 0.0, one[...])
    send[COLS : COLS + 8, :] = jnp.where(low[0:8], own, one[0:8, :])


def fold1_kernel(got, leaf_part, send, zero, one):
    fold_rows(got, COLS + 1, send, zero, one)
    send[2 * COLS : 3 * COLS, :] = leaf_part[...]


def fold2_kernel(got, send, zero, one):
    fold_rows(got, COLS + 3, send, zero, one)


def send_rows(send, coefs, rows):
    for r in range(COLS):
        send[r] = coefs[r : r + 1, :]
    for k, row in enumerate(rows):
        send[COLS + k] = row


def sum_tiles(got, first):
    return [
        tree_sum([got[4 * y + x, at : at + COLS] for x in range(4)]) for at in (first, first + COLS) for y in range(4)
    ]


def column_directions(marks, table, leaf_parts, got0, directions):
    low = lane((COLS, PTS)) < RANK
    odd = marks[NG : NG + 1, :] > 0.5
    top = tree_sum(table[0:4])
    for y in range(4):
        coefs = jnp.where(low, top, jnp.where(odd, table[4 + y], table[y]))
        high = coefs.astype(BF16)
        both = jnp.concatenate([high, (coefs - high.astype(F32)).astype(BF16)], 0)
        for j in range(4 * y, 4 * y + 4):
            bases = got0[j, BASES]
            first = bases.astype(BF16)
            r = jnp.dot(both, first, preferred_element_type=F32)
            r = r[0:COLS] + r[COLS:] + jnp.dot(high, (bases - first.astype(F32)).astype(BF16), preferred_element_type=F32)
            directions[j] = leaf_parts(j) + r


def own_direction(marks, directions):
    return tree_sum([directions[j] * marks[j : j + 1, :] for j in range(NG)])


def features(x, left):
    def pieces(v):
        first = v.astype(BF16).astype(F32)
        second = (v - first).astype(BF16).astype(F32)
        third = (v - first - second).astype(BF16).astype(F32)
        return first, second, third

    a, b, c = pieces(x)
    norms = pieces(jnp.sum(x * x, 0, keepdims=True))
    ones = (jnp.ones((1, PTS), F32),) * 3
    if left:
        parts = [a, a, b, b, a, c]
        tail = tile_rows(norms + ones)
    else:
        a, b, c = -2.0 * a, -2.0 * b, -2.0 * c
        parts = [a, b, a, b, c, a]
        tail = tile_rows(ones + norms)
    return jnp.concatenate(parts + [tail, jnp.zeros((PTS - 6 * COLS - 8, PTS), F32)], 0)


def first_kernel(marks, got_a, got_b, high, low, out, z, table, directions, left_f, right_f, both, acc):
    tops = [tree_sum([got_a[4 * y + x, COLS : 2 * COLS] for x in range(4)]) for y in range(4)]
    subs = [tree_sum([got_a[4 * y + x, 2 * COLS : 5 * COLS // 2] for x in range(4)]) for y in range(4)]
    now = tops + [unpack_half(v) for v in subs]
    for t in range(NT):
        table[t] = now[t]
    column_directions(marks, now, lambda j: got_a[j, LEAF_PART], got_a, directions)
    z[...] = own_direction(marks, directions)
    for j in range(NG):
        at = slice(j * PTS, (j + 1) * PTS)
        right_f[:, at] = features(got_b[j, 0:COLS] * COORD_SCALE, False).astype(BF16)
        left_f[at, :] = features(got_a[j, 0:COLS] * COORD_SCALE, True).T.astype(BF16)
        v = directions[j] * LEAD
        v_high = v.astype(BF16)
        both[j] = jnp.concatenate([v_high, (v - v_high.astype(F32)).astype(BF16)], 0)
    acc[...] = jnp.zeros_like(acc)
    height, width = 1024, 256
    blocks = height // PTS

    def step(i, carry):
        rows = pl.ds(pl.multiple_of(i * height, height), height)
        points = left_f[rows, :]
        vectors = jnp.concatenate([both[i * blocks + b] for b in range(blocks)], 1)
        for j in range(0, NG * PTS, width):
            s = jnp.dot(points, right_f[:, j : j + width], preferred_element_type=F32)
            s = jnp.maximum(s, 1e-30)
            v = s * lax.rsqrt(s)
            w = v + SHIFT
            k = (w * w + REST) * jnp.exp2(-v)
            k_high = k.astype(BF16)
            k_low = (k - k_high.astype(F32)).astype(BF16)
            high[rows, j : j + width] = k_high
            low[rows, j : j + width] = k_low
            r = jnp.dot(vectors, k_high, preferred_element_type=F32)
            r = r[0:COLS] + r[COLS:] + jnp.dot(vectors[0:COLS], k_low, preferred_element_type=F32)
            acc[:, j : j + width] += r
        return carry

    lax.fori_loop(0, NG // blocks, step, 0)
    for b in range(NG):
        out[b] = acc[:, b * PTS : (b + 1) * PTS]


def matvec(directions, high, low, out):
    v = jnp.concatenate([directions[j] * LEAD for j in range(NG)], 1)
    v_high = v.astype(BF16)
    both = jnp.concatenate([v_high, (v - v_high.astype(F32)).astype(BF16)], 0)
    width = 512
    for j in range(0, NG * PTS, width):
        r = jnp.dot(both, high[:, j : j + width], preferred_element_type=F32)
        r = r[0:COLS] + r[COLS:] + jnp.dot(v_high, low[:, j : j + width], preferred_element_type=F32)
        for b in range(width // PTS):
            out[j // PTS + b] = r[:, b * PTS : (b + 1) * PTS]


def image0_kernel(got, z, rhs, basis, leaf, q, leaf_part, send):
    q[...] = tree_sum([got[j] for j in range(NG)]) + NOISE * z[...]
    send_rows(send, dot_nt(q[...], basis[...]), [pack([rowdot(rhs[...], z[...]), rowdot(z[...], q[...])])])
    leaf_part[...] = dot_nt(q[...], leaf[...])


def second_kernel(
    marks, got, got0, table0, rhs, q, leaf_rhs, leaf_q, high, low, out, z, res, leaf_res, table, table_q, sums, directions
):
    now = sum_tiles(got, 0)
    total = tree_sum(now[4:8])
    sums[...] = total[0:8]
    alpha = unpack(total[0:1], 0) / unpack(total[0:1], 1)
    for t in range(NT):
        table_q[t] = now[t]
        now[t] = table0[t] - alpha * now[t]
        table[t] = now[t]
    column_directions(
        marks, now, lambda j: got0[j, LEAF_PART] - alpha * got[j, 2 * COLS : 3 * COLS], got0, directions
    )
    z[...] = own_direction(marks, directions)
    res[...] = rhs[...] - alpha * q[...]
    leaf_res[...] = leaf_rhs[...] - alpha * leaf_q[...]
    matvec(directions, high, low, out)


def image1_kernel(got, z1, z0, res, q, leaf_res, leaf_q, leaf, basis, p, send):
    p[...] = tree_sum([got[j] for j in range(NG)]) + NOISE * z1[...]
    rv, qv, pv, zv = res[...], q[...], p[...], z1[...]
    rb, qb, pb = leaf_res[...], leaf_q[...], dot_nt(pv, leaf[...])
    rows = [
        pack([rowdot(rv, zv), rowdot(zv, pv), rowdot(zv, qv), rowdot(z0[...], pv)]),
        pack([rowdot(rv, rb), rowdot(rv, qb), rowdot(rv, pb)]),
        pack([rowdot(qv, qb), rowdot(qv, pb), rowdot(pv, pb)]),
    ]
    send_rows(send, dot_nt(pv, basis[...]), rows)


def finish_kernel(got, z0, z1, res, q, p, table1, table_q, sums0, x_out, r_out, coefs):
    now = sum_tiles(got, 0)
    sums = tree_sum(now[4:8])
    rz0, z0q = unpack(sums0[0:1, :], 0), unpack(sums0[0:1, :], 1)
    rz1, z1p, z1q, z0p = (unpack(sums[0:1], k) for k in range(4))
    rbr, rbq, rbp = (unpack(sums[1:2], k) for k in range(3))
    qbq, qbp, pbp = (unpack(sums[2:3], k) for k in range(3))
    alpha0 = rz0 / z0q
    beta0 = rz1 / rz0
    alpha1 = rz1 / (z1p + beta0 * (z1q + z0p) + beta0 * beta0 * z0q)
    image = p[...] + beta0 * q[...]
    r_out[...] = res[...] - alpha1 * image
    x_out[...] = alpha0 * z0[...] + alpha1 * (z1[...] + beta0 * z0[...])
    leaf_part = (
        rbr
        - 2.0 * alpha1 * (rbp + beta0 * rbq)
        + alpha1 * alpha1 * (pbp + 2.0 * beta0 * qbp + beta0 * beta0 * qbq)
    )
    low = lane((COLS, PTS)) < RANK
    now = [table1[t] - alpha1 * (now[t] + beta0 * table_q[t]) for t in range(NT)]
    top = jnp.where(low, tree_sum(now[0:4]), 0.0)
    squares = top * top + tree_sum([jnp.where(low, 0.0, v * v) for v in now])
    beta1 = (leaf_part + jnp.sum(squares, 1, keepdims=True)) / rz1
    for k, v in enumerate((alpha0, alpha1, beta0, beta1)):
        coefs[k // 2, k % 2 : k % 2 + 1, :] = pack([v])[:, 0:COLS]


def gather(block, axes):
    return lax.all_to_all(jnp.broadcast_to(block[None], (NG,) + block.shape), axes, 0, 0, tiled=True)


def scatter(parts):
    return lax.all_to_all(parts, GB, 0, 0, tiled=True)


def on_device(points, inverse_length, target, probe_bits, leaf_inverse, top_basis, sub_basis):
    vec = ((COLS, PTS), F32)
    square = ((PTS, PTS), F32)
    table = ((NT, COLS, PTS), F32)
    block = ((NG * PTS, NG * PTS), BF16)
    parts = ((NG, COLS, PTS), F32)
    rows1 = ((COLS + 1, 1, PTS), F32)
    rows2 = ((COLS + 3, 1, PTS), F32)
    two = [pltpu.VMEM((COLS, PTS), F32)] * 2
    dma = pltpu.SemaphoreType.DMA
    where = lax.axis_index(("zl",) + GA).astype(jnp.int32).reshape(1)
    send, rhs, basis, leaf, leaf_part, marks = call(
        start_kernel,
        [((2 * COLS, PTS), F32), vec, square, square, vec, ((NG + 8, PTS), F32)],
        where, inverse_length, points, target[None, :], probe_bits, top_basis, sub_basis, leaf_inverse,
        spaces=[SMEM] + [HBM] * 7,
        scratch=[
            pltpu.VMEM((COLS, PTS), F32), pltpu.VMEM((1, PTS), F32), pltpu.VMEM((COLS - 1, PTS), jnp.int32),
            pltpu.SMEM((COLS,), F32), dma((7,)),
        ],
        name="start",
    )
    got_b = gather(send, GB)
    (send,) = call(fold0_kernel, [((SEND0, PTS), F32)], got_b, send, basis, leaf_part, name="fold0")
    got_a = gather(send, GA)
    high, low, out, z0, table0 = call(
        first_kernel, [block, block, parts, vec, table], marks, got_a, got_b, limit=24 << 20,
        scratch=[
            pltpu.VMEM((NG, COLS, PTS), F32), pltpu.VMEM((NG * PTS, PTS), BF16), pltpu.VMEM((PTS, NG * PTS), BF16),
            pltpu.VMEM((NG, 2 * COLS, PTS), BF16), pltpu.VMEM((COLS, NG * PTS), F32),
        ],
        name="first",
    )
    q, leaf_q, send = call(image0_kernel, [vec, vec, rows1], scatter(out), z0, rhs, basis, leaf, name="image0")
    (send,) = call(fold1_kernel, [((3 * COLS, PTS), F32)], gather(send, GB), leaf_q, scratch=two, name="fold1")
    out, z1, res, leaf_res, table1, table_q, sums0 = call(
        second_kernel, [parts, vec, vec, vec, table, table, ((8, PTS), F32)],
        marks, gather(send, GA), got_a, table0, rhs, q, leaf_part, leaf_q, high, low,
        limit=24 << 20, scratch=[pltpu.VMEM((NG, COLS, PTS), F32)], name="second",
    )
    p, send = call(
        image1_kernel, [vec, rows2], scatter(out), z1, z0, res, q, leaf_res, leaf_q, leaf, basis, name="image1"
    )
    (send,) = call(fold2_kernel, [((2 * COLS, PTS), F32)], gather(send, GB), scratch=two, name="fold2")
    x_out, r_out, coefs = call(
        finish_kernel, [vec, vec, ((2, 2, COLS), F32)],
        gather(send, GA), z0, z1, res, q, p, table1, table_q, sums0, name="finish",
    )
    return x_out, r_out, coefs


def solution(mesh):
    named = Mesh(mesh.devices.reshape(2, 4, 4, 4, 2), AXES)
    return jax.shard_map(
        on_device,
        mesh=named,
        in_specs=(P(None, AXES), P(), P(AXES), P(None, AXES), P(AXES, None), P(None, AXES), P(None, AXES)),
        out_specs=(P(None, AXES), P(None, AXES), P()),
        check_vma=False,
    )
```

```python
import functools
import math

import jax
import jax.numpy as jnp
from jax import lax
from jax.experimental import pallas as pl
from jax.experimental.pallas import tpu as pltpu
from jax.sharding import Mesh
from jax.sharding import PartitionSpec as P

AXES = ("zl", "y", "zh", "x", "c")
GA = ("y", "x")
GB = ("zl", "zh", "c")
NG = 16
NT = 8
COLS = 16
PTS = 128
RANK = 64
NOISE = 0.5
F32 = jnp.float32
BF16 = jnp.bfloat16
LN2 = math.log(2.0)
COORD_SCALE = math.sqrt(5.0) / LN2
LEAD = LN2 * LN2 / 3.0
SHIFT = 1.5 / LN2
REST = 1.0 / LEAD - SHIFT * SHIFT
HIGHEST = lax.Precision.HIGHEST


def dot_nt(a, b):
    return lax.dot_general(a, b, (((1,), (1,)), ((), ())), precision=HIGHEST, preferred_element_type=F32)


def dot_nn(a, b):
    return lax.dot_general(a, b, (((1,), (0,)), ((), ())), precision=HIGHEST, preferred_element_type=F32)


def lane(shape):
    return lax.broadcasted_iota(jnp.int32, shape, 1)


def sublane(shape):
    return lax.broadcasted_iota(jnp.int32, shape, 0)


def pack(sums):
    shape = (COLS, PTS)
    acc = jnp.zeros(shape, F32)
    for k, s in enumerate(sums):
        acc = jnp.where(lane(shape) == COLS * k + sublane(shape), jnp.broadcast_to(s, shape), acc)
    return jnp.sum(acc, 0, keepdims=True)


def unpack(row, k):
    shape = (COLS, PTS)
    hit = lane(shape) == COLS * k + sublane(shape)
    return jnp.sum(jnp.where(hit, jnp.broadcast_to(row, shape), 0.0), 1, keepdims=True)


def rowdot(a, b):
    return jnp.sum(a * b, 1, keepdims=True)


def tile_rows(rows):
    shape = (8, PTS)
    out = jnp.zeros(shape, F32)
    for k, r in enumerate(rows):
        out = jnp.where(sublane(shape) == k, jnp.broadcast_to(r, shape), out)
    return out


def tree_sum(terms):
    terms = list(terms)
    while len(terms) > 1:
        terms = [terms[i] + terms[i + 1] if i + 1 < len(terms) else terms[i] for i in range(0, len(terms), 2)]
    return terms[0]


VMEM = pltpu.MemorySpace.VMEM
SMEM = pltpu.MemorySpace.SMEM
HBM = pltpu.MemorySpace.HBM


def call(kernel, outs, *args, spaces=None, out_spaces=None, limit=8 << 20, scratch=(), name=None):
    spaces = spaces or [VMEM] * len(args)
    out_spaces = out_spaces or [VMEM] * len(outs)
    args = [pltpu.with_memory_space_constraint(a, m) if m is HBM else a for a, m in zip(args, spaces)]
    return pl.pallas_call(
        kernel,
        out_shape=[m(s, d) if m is HBM else jax.ShapeDtypeStruct(s, d) for m, (s, d) in zip(out_spaces, outs)],
        in_specs=[pl.BlockSpec(memory_space=m) for m in spaces],
        out_specs=[pl.BlockSpec(memory_space=m) for m in out_spaces],
        scratch_shapes=list(scratch),
        compiler_params=pltpu.CompilerParams(vmem_limit_bytes=limit),
        name=name,
    )(*args)


HALF = COLS // 2
COEFS = COLS + HALF
SEND0 = 5 * COLS // 2 + PTS + COLS
BASES = slice(5 * COLS // 2, 5 * COLS // 2 + PTS)
LEAF_PART = slice(SEND0 - COLS, SEND0)


def start_kernel(where, inv_h, points_h, target_h, bits_h, top_h, sub_h, leaf_h, send, rhs, basis, leaf, leaf_part, marks, points, target, bits, inv, sems):
    moves = [
        pltpu.make_async_copy(src, dst, sems.at[k])
        for k, (src, dst) in enumerate(
            [
                (bits_h, bits),
                (target_h, target),
                (top_h, basis.at[pl.ds(0, RANK)]),
                (sub_h, basis.at[pl.ds(RANK, RANK)]),
                (points_h, points),
                (inv_h, inv),
                (leaf_h, leaf),
            ]
        )
    ]
    for m in moves:
        m.start()
    row = sublane((NG + 8, PTS))
    place = where[0]
    hit = (row == lax.rem(place, NG)) | ((row >= NG) & (place >= NG))
    marks[...] = jnp.where(hit, 1.0, 0.0)
    for m in moves[4:6]:
        m.wait()
    scale = jnp.zeros((COLS, PTS), F32)
    for k in range(COLS):
        scale = jnp.where(sublane((COLS, PTS)) == k, inv[k], scale)
    send[0:COLS, :] = points[...] * scale
    for m in moves[0:2]:
        m.wait()
    rhs[0:1, :] = target[...]
    rhs[1:COLS, :] = 2.0 * bits[...].astype(F32) - 1.0
    for m in moves[2:4]:
        m.wait()
    send[COLS : 2 * COLS, :] = dot_nt(rhs[...], basis[...])
    moves[6].wait()
    leaf_part[...] = dot_nt(rhs[...], leaf[...])


def pack_half(tile):
    return jnp.where(lane((8, PTS)) < RANK, pltpu.roll(tile[0:8], RANK, 1), tile[8:16])


def unpack_half(packed):
    return jnp.concatenate([pltpu.roll(packed, RANK, 1), packed], 0)


def fold0_kernel(got, own, basis, leaf_part, send):
    low = lane((COLS, PTS)) < RANK
    zero = tree_sum([got[j, COLS : 2 * COLS] for j in range(NG // 2)])
    one = tree_sum([got[j, COLS : 2 * COLS] for j in range(NG // 2, NG)])
    send[0:COLS, :] = own[0:COLS, :]
    send[COLS : 2 * COLS, :] = jnp.where(low, zero + one, zero)
    send[2 * COLS : 5 * COLS // 2, :] = pack_half(one)
    send[BASES, :] = basis[...]
    send[LEAF_PART, :] = leaf_part[...]


def fold_rows(got, scalars, send, zero, one):
    for r in range(COLS):
        zero[r : r + 1, :] = tree_sum([got[j, r] for j in range(NG // 2)])
        one[r : r + 1, :] = tree_sum([got[j, r] for j in range(NG // 2, NG)])
    low = lane((COLS, PTS)) < RANK
    send[0:COLS, :] = jnp.where(low, zero[...] + one[...], zero[...])
    send[COLS:COEFS, :] = pack_half(one[...])
    for k in range(scalars):
        send[COEFS + k : COEFS + k + 1, :] = tree_sum([got[j, COLS + k] for j in range(NG)])


def fold1_kernel(got, leaf_part, send, zero, one):
    fold_rows(got, 1, send, zero, one)
    send[COEFS + 1 :, :] = leaf_part[...]


def fold2_kernel(got, send, zero, one):
    fold_rows(got, 2, send, zero, one)


def send_rows(send, coefs, rows):
    send[0:COLS, :] = coefs
    for k, row in enumerate(rows):
        send[COLS + k : COLS + k + 1, :] = row


def sum_rows(got, scalars, held):
    for y in range(4):
        for r in range(COEFS):
            held[y, r : r + 1, :] = tree_sum([got[4 * y + x, r] for x in range(4)])
    table = [held[y, 0:COLS] for y in range(4)] + [unpack_half(held[y, COLS:COEFS]) for y in range(4)]
    return table, [tree_sum([got[j, COEFS + k] for j in range(NG)]) for k in range(scalars)]


def column_directions(marks, table, leaf_parts, got0, directions):
    low = lane((COLS, PTS)) < RANK
    odd = marks[NG : NG + 1, :] > 0.5
    top = tree_sum(table[0:4])
    for y in range(4):
        coefs = jnp.where(low, top, jnp.where(odd, table[4 + y], table[y]))
        high = coefs.astype(BF16)
        both = jnp.concatenate([high, (coefs - high.astype(F32)).astype(BF16)], 0)
        for j in range(4 * y, 4 * y + 4):
            bases = got0[j, BASES]
            first = bases.astype(BF16)
            r = jnp.dot(both, first, preferred_element_type=F32)
            r = r[0:COLS] + r[COLS:] + jnp.dot(high, (bases - first.astype(F32)).astype(BF16), preferred_element_type=F32)
            directions[j] = leaf_parts(j) + r


def own_direction(marks, directions):
    return tree_sum([directions[j] * marks[j : j + 1, :] for j in range(NG)])


def features(x, left):
    def pieces(v):
        first = v.astype(BF16).astype(F32)
        second = (v - first).astype(BF16).astype(F32)
        third = (v - first - second).astype(BF16).astype(F32)
        return first, second, third

    a, b, c = pieces(x)
    norms = pieces(jnp.sum(x * x, 0, keepdims=True))
    ones = (jnp.ones((1, PTS), F32),) * 3
    if left:
        parts = [a, a, b, b, a, c]
        tail = tile_rows(norms + ones)
    else:
        a, b, c = -2.0 * a, -2.0 * b, -2.0 * c
        parts = [a, b, a, b, c, a]
        tail = tile_rows(ones + norms)
    return jnp.concatenate(parts + [tail, jnp.zeros((PTS - 6 * COLS - 8, PTS), F32)], 0)


def first_kernel(marks, got_a, got_b, high, low, out, z, table, directions, left_f, right_f, both):
    tops = [tree_sum([got_a[4 * y + x, COLS : 2 * COLS] for x in range(4)]) for y in range(4)]
    subs = [tree_sum([got_a[4 * y + x, 2 * COLS : 5 * COLS // 2] for x in range(4)]) for y in range(4)]
    now = tops + [unpack_half(v) for v in subs]
    for t in range(NT):
        table[t] = now[t]
    column_directions(marks, now, lambda j: got_a[j, LEAF_PART], got_a, directions)
    z[...] = own_direction(marks, directions)
    for j in range(NG):
        at = slice(j * PTS, (j + 1) * PTS)
        right_f[:, at] = features(got_b[j, 0:COLS] * COORD_SCALE, False).astype(BF16)
        left_f[at, :] = features(got_a[j, 0:COLS] * COORD_SCALE, True).T.astype(BF16)
        v = directions[j] * LEAD
        v_high = v.astype(BF16)
        both[j] = jnp.concatenate([v_high, (v - v_high.astype(F32)).astype(BF16)], 0)
    points = left_f[...]
    vectors = jnp.concatenate([both[j] for j in range(NG)], 1)
    width = 256
    for j in range(0, NG * PTS, width):
        s = jnp.dot(points, right_f[:, j : j + width], preferred_element_type=F32)
        s = jnp.maximum(s, 1e-30)
        v = s * lax.rsqrt(s)
        w = v + SHIFT
        k = (w * w + REST) * jnp.exp2(-v)
        k_high = k.astype(BF16)
        k_low = (k - k_high.astype(F32)).astype(BF16)
        high[:, j : j + width] = k_high
        low[:, j : j + width] = k_low
        r = jnp.dot(vectors, k_high, preferred_element_type=F32)
        r = r[0:COLS] + r[COLS:] + jnp.dot(vectors[0:COLS], k_low, preferred_element_type=F32)
        for b in range(width // PTS):
            out[j // PTS + b] = r[:, b * PTS : (b + 1) * PTS]


def matvec(directions, high, low, out):
    v = jnp.concatenate([directions[j] * LEAD for j in range(NG)], 1)
    v_high = v.astype(BF16)
    both = jnp.concatenate([v_high, (v - v_high.astype(F32)).astype(BF16)], 0)
    width = 512
    for j in range(0, NG * PTS, width):
        r = jnp.dot(both, high[:, j : j + width], preferred_element_type=F32)
        r = r[0:COLS] + r[COLS:] + jnp.dot(v_high, low[:, j : j + width], preferred_element_type=F32)
        for b in range(width // PTS):
            out[j // PTS + b] = r[:, b * PTS : (b + 1) * PTS]


def image0_kernel(got, z, rhs, basis, leaf, q, leaf_part, send):
    q[...] = tree_sum([got[j] for j in range(NG)]) + NOISE * z[...]
    send_rows(send, dot_nt(q[...], basis[...]), [pack([rowdot(rhs[...], z[...]), rowdot(z[...], q[...])])])
    leaf_part[...] = dot_nt(q[...], leaf[...])


def second_kernel(
    marks, got, got0, table0, rhs, q, leaf_rhs, leaf_q, high, low,
    out, z, res, leaf_res, table, table_q, sums, directions, held, leaf_parts,
):
    now, (total,) = sum_rows(got, 1, held)
    for j in range(NG):
        for r in range(COLS):
            leaf_parts[j, r : r + 1, :] = got[j, COEFS + 1 + r]
    sums[...] = total
    alpha = unpack(total, 0) / unpack(total, 1)
    for t in range(NT):
        table_q[t] = now[t]
        now[t] = table0[t] - alpha * now[t]
        table[t] = now[t]
    column_directions(
        marks, now, lambda j: got0[j, LEAF_PART] - alpha * leaf_parts[j], got0, directions
    )
    z[...] = own_direction(marks, directions)
    res[...] = rhs[...] - alpha * q[...]
    leaf_res[...] = leaf_rhs[...] - alpha * leaf_q[...]
    matvec(directions, high, low, out)


def image1_kernel(got, z1, z0, res, q, leaf_res, leaf_q, leaf, basis, p, send):
    p[...] = tree_sum([got[j] for j in range(NG)]) + NOISE * z1[...]
    rv, qv, pv, zv = res[...], q[...], p[...], z1[...]
    rb, qb, pb = leaf_res[...], leaf_q[...], dot_nt(pv, leaf[...])
    rows = [
        pack(
            [
                rowdot(rv, zv), rowdot(zv, pv), rowdot(zv, qv), rowdot(z0[...], pv),
                rowdot(rv, rb), rowdot(rv, qb), rowdot(rv, pb), rowdot(qv, qb),
            ]
        ),
        pack([rowdot(qv, pb), rowdot(pv, pb)]),
    ]
    send_rows(send, dot_nt(pv, basis[...]), rows)


def finish_kernel(got, z0, z1, res, q, p, table1, table_q, sums0, x_h, r_h, coefs, x_out, r_out, sems, held):
    now, (sums, more) = sum_rows(got, 2, held)
    rz0, z0q = unpack(sums0[...], 0), unpack(sums0[...], 1)
    rz1, z1p, z1q, z0p, rbr, rbq, rbp, qbq = (unpack(sums, k) for k in range(8))
    qbp, pbp = unpack(more, 0), unpack(more, 1)
    alpha0 = rz0 / z0q
    beta0 = rz1 / rz0
    alpha1 = rz1 / (z1p + beta0 * (z1q + z0p) + beta0 * beta0 * z0q)
    image = p[...] + beta0 * q[...]
    r_out[...] = res[...] - alpha1 * image
    x_out[...] = alpha0 * z0[...] + alpha1 * (z1[...] + beta0 * z0[...])
    moves = (pltpu.make_async_copy(r_out, r_h, sems.at[0]), pltpu.make_async_copy(x_out, x_h, sems.at[1]))
    for m in moves:
        m.start()
    leaf_part = (
        rbr
        - 2.0 * alpha1 * (rbp + beta0 * rbq)
        + alpha1 * alpha1 * (pbp + 2.0 * beta0 * qbp + beta0 * beta0 * qbq)
    )
    low = lane((COLS, PTS)) < RANK
    now = [table1[t] - alpha1 * (now[t] + beta0 * table_q[t]) for t in range(NT)]
    top = jnp.where(low, tree_sum(now[0:4]), 0.0)
    squares = top * top + tree_sum([jnp.where(low, 0.0, v * v) for v in now])
    beta1 = (leaf_part + jnp.sum(squares, 1, keepdims=True)) / rz1
    for k, v in enumerate((alpha0, alpha1, beta0, beta1)):
        coefs[k // 2, k % 2 : k % 2 + 1, :] = pack([v])[:, 0:COLS]
    for m in moves:
        m.wait()


def gather(block, axes):
    return lax.all_to_all(jnp.broadcast_to(block[None], (NG,) + block.shape), axes, 0, 0, tiled=True)


def scatter(parts):
    return lax.all_to_all(parts, GB, 0, 0, tiled=True)


def on_device(points, inverse_length, target, probe_bits, leaf_inverse, top_basis, sub_basis):
    vec = ((COLS, PTS), F32)
    square = ((PTS, PTS), F32)
    table = ((NT, COLS, PTS), F32)
    block = ((NG * PTS, NG * PTS), BF16)
    parts = ((NG, COLS, PTS), F32)
    rows1 = ((COLS + 1, PTS), F32)
    rows2 = ((COLS + 2, PTS), F32)
    held = pltpu.VMEM((4, COEFS, PTS), F32)
    two = [pltpu.VMEM((COLS, PTS), F32)] * 2
    dma = pltpu.SemaphoreType.DMA
    where = lax.axis_index(("zl",) + GA).astype(jnp.int32).reshape(1)
    send, rhs, basis, leaf, leaf_part, marks = call(
        start_kernel,
        [((2 * COLS, PTS), F32), vec, square, square, vec, ((NG + 8, PTS), F32)],
        where, inverse_length, points, target[None, :], probe_bits, top_basis, sub_basis, leaf_inverse,
        spaces=[SMEM] + [HBM] * 7,
        scratch=[
            pltpu.VMEM((COLS, PTS), F32), pltpu.VMEM((1, PTS), F32), pltpu.VMEM((COLS - 1, PTS), jnp.int32),
            pltpu.SMEM((COLS,), F32), dma((7,)),
        ],
        name="start",
    )
    got_b = gather(send, GB)
    (send,) = call(fold0_kernel, [((SEND0, PTS), F32)], got_b, send, basis, leaf_part, name="fold0")
    got_a = gather(send, GA)
    high, low, out, z0, table0 = call(
        first_kernel, [block, block, parts, vec, table], marks, got_a, got_b, limit=24 << 20,
        scratch=[
            pltpu.VMEM((NG, COLS, PTS), F32), pltpu.VMEM((NG * PTS, PTS), BF16), pltpu.VMEM((PTS, NG * PTS), BF16),
            pltpu.VMEM((NG, 2 * COLS, PTS), BF16),
        ],
        name="first",
    )
    q, leaf_q, send = call(image0_kernel, [vec, vec, rows1], scatter(out), z0, rhs, basis, leaf, name="image0")
    (send,) = call(fold1_kernel, [((COEFS + 1 + COLS, PTS), F32)], gather(send[:, None], GB), leaf_q, scratch=two, name="fold1")
    out, z1, res, leaf_res, table1, table_q, sums0 = call(
        second_kernel, [parts, vec, vec, vec, table, table, ((1, PTS), F32)],
        marks, gather(send[:, None], GA), got_a, table0, rhs, q, leaf_part, leaf_q, high, low,
        limit=24 << 20,
        scratch=[pltpu.VMEM((NG, COLS, PTS), F32), held, pltpu.VMEM((NG, COLS, PTS), F32)], name="second",
    )
    p, send = call(
        image1_kernel, [vec, rows2], scatter(out), z1, z0, res, q, leaf_res, leaf_q, leaf, basis, name="image1"
    )
    (send,) = call(fold2_kernel, [((COEFS + 2, PTS), F32)], gather(send[:, None], GB), scratch=two, name="fold2")
    x_out, r_out, coefs = call(
        finish_kernel, [vec, vec, ((2, 2, COLS), F32)],
        gather(send[:, None], GA), z0, z1, res, q, p, table1, table_q, sums0,
        out_spaces=[HBM, HBM, VMEM], scratch=two + [dma((2,)), held], name="finish",
    )
    return x_out, r_out, coefs


def solution(mesh):
    named = Mesh(mesh.devices.reshape(2, 4, 4, 4, 2), AXES)
    return jax.shard_map(
        on_device,
        mesh=named,
        in_specs=(P(None, AXES), P(), P(AXES), P(None, AXES), P(AXES, None), P(None, AXES), P(None, AXES)),
        out_specs=(P(None, AXES), P(None, AXES), P()),
        check_vma=False,
    )
```

```python
import functools
import math

import jax
import jax.numpy as jnp
from jax import lax
from jax.experimental import pallas as pl
from jax.experimental.pallas import tpu as pltpu
from jax.sharding import Mesh
from jax.sharding import PartitionSpec as P

AXES = ("zl", "y", "zh", "x", "c")
GA = ("y", "x")
GB = ("zl", "zh", "c")
NG = 16
NT = 8
COLS = 16
PTS = 128
RANK = 64
NOISE = 0.5
F32 = jnp.float32
BF16 = jnp.bfloat16
LN2 = math.log(2.0)
COORD_SCALE = math.sqrt(5.0) / LN2
LEAD = LN2 * LN2 / 3.0
SHIFT = 1.5 / LN2
REST = 1.0 / LEAD - SHIFT * SHIFT
HIGHEST = lax.Precision.HIGHEST


def dot_nt(a, b):
    return lax.dot_general(a, b, (((1,), (1,)), ((), ())), precision=HIGHEST, preferred_element_type=F32)


def dot_nn(a, b):
    return lax.dot_general(a, b, (((1,), (0,)), ((), ())), precision=HIGHEST, preferred_element_type=F32)


def lane(shape):
    return lax.broadcasted_iota(jnp.int32, shape, 1)


def sublane(shape):
    return lax.broadcasted_iota(jnp.int32, shape, 0)


def pack(sums):
    shape = (COLS, PTS)
    acc = jnp.zeros(shape, F32)
    for k, s in enumerate(sums):
        acc = jnp.where(lane(shape) == COLS * k + sublane(shape), jnp.broadcast_to(s, shape), acc)
    return jnp.sum(acc, 0, keepdims=True)


def unpack(row, k):
    shape = (COLS, PTS)
    hit = lane(shape) == COLS * k + sublane(shape)
    return jnp.sum(jnp.where(hit, jnp.broadcast_to(row, shape), 0.0), 1, keepdims=True)


def rowdot(a, b):
    return jnp.sum(a * b, 1, keepdims=True)


def tile_rows(rows):
    shape = (8, PTS)
    out = jnp.zeros(shape, F32)
    for k, r in enumerate(rows):
        out = jnp.where(sublane(shape) == k, jnp.broadcast_to(r, shape), out)
    return out


def tree_sum(terms):
    terms = list(terms)
    while len(terms) > 1:
        terms = [terms[i] + terms[i + 1] if i + 1 < len(terms) else terms[i] for i in range(0, len(terms), 2)]
    return terms[0]


VMEM = pltpu.MemorySpace.VMEM
SMEM = pltpu.MemorySpace.SMEM
HBM = pltpu.MemorySpace.HBM


def call(kernel, outs, *args, spaces=None, out_spaces=None, limit=8 << 20, scratch=(), name=None):
    spaces = spaces or [VMEM] * len(args)
    out_spaces = out_spaces or [VMEM] * len(outs)
    args = [pltpu.with_memory_space_constraint(a, m) if m is HBM else a for a, m in zip(args, spaces)]
    return pl.pallas_call(
        kernel,
        out_shape=[m(s, d) if m is HBM else jax.ShapeDtypeStruct(s, d) for m, (s, d) in zip(out_spaces, outs)],
        in_specs=[pl.BlockSpec(memory_space=m) for m in spaces],
        out_specs=[pl.BlockSpec(memory_space=m) for m in out_spaces],
        scratch_shapes=list(scratch),
        compiler_params=pltpu.CompilerParams(vmem_limit_bytes=limit),
        name=name,
    )(*args)


HALF = COLS // 2
COEFS = COLS + HALF
SEND0 = 5 * COLS // 2 + PTS + COLS
BASES = slice(5 * COLS // 2, 5 * COLS // 2 + PTS)
LEAF_PART = slice(SEND0 - COLS, SEND0)


def start_kernel(where, inv_h, points_h, target_h, bits_h, top_h, sub_h, leaf_h, send, rhs, basis, leaf, leaf_part, marks, points, target, bits, inv, sems):
    moves = [
        pltpu.make_async_copy(src, dst, sems.at[k])
        for k, (src, dst) in enumerate(
            [
                (bits_h, bits),
                (target_h, target),
                (top_h, basis.at[pl.ds(0, RANK)]),
                (sub_h, basis.at[pl.ds(RANK, RANK)]),
                (points_h, points),
                (inv_h, inv),
                (leaf_h, leaf),
            ]
        )
    ]
    for m in moves:
        m.start()
    row = sublane((NG + 8, PTS))
    place = where[0]
    hit = (row == lax.rem(place, NG)) | ((row >= NG) & (place >= NG))
    marks[...] = jnp.where(hit, 1.0, 0.0)
    for m in moves:
        m.wait()
    scale = jnp.zeros((COLS, PTS), F32)
    for k in range(COLS):
        scale = jnp.where(sublane((COLS, PTS)) == k, inv[k], scale)
    rhs[0:1, :] = target[...]
    rhs[1:COLS, :] = 2.0 * bits[...].astype(F32) - 1.0
    send[0:COLS, :] = points[...] * scale
    send[COLS : 2 * COLS, :] = dot_nt(rhs[...], basis[...])
    leaf_part[...] = dot_nt(rhs[...], leaf[...])


def pack_half(tile):
    return jnp.where(lane((8, PTS)) < RANK, pltpu.roll(tile[0:8], RANK, 1), tile[8:16])


def unpack_half(packed):
    return jnp.concatenate([pltpu.roll(packed, RANK, 1), packed], 0)


def fold0_kernel(got, own, basis, leaf_part, send):
    low = lane((COLS, PTS)) < RANK
    zero = tree_sum([got[j, COLS : 2 * COLS] for j in range(NG // 2)])
    one = tree_sum([got[j, COLS : 2 * COLS] for j in range(NG // 2, NG)])
    send[0:COLS, :] = own[0:COLS, :]
    send[COLS : 2 * COLS, :] = jnp.where(low, zero + one, zero)
    send[2 * COLS : 5 * COLS // 2, :] = pack_half(one)
    send[BASES, :] = basis[...]
    send[LEAF_PART, :] = leaf_part[...]


def fold_rows(got, scalars, send, zero, one):
    for r in range(COLS):
        zero[r : r + 1, :] = tree_sum([got[j, r] for j in range(NG // 2)])
        one[r : r + 1, :] = tree_sum([got[j, r] for j in range(NG // 2, NG)])
    low = lane((COLS, PTS)) < RANK
    send[0:COLS, :] = jnp.where(low, zero[...] + one[...], zero[...])
    send[COLS:COEFS, :] = pack_half(one[...])
    for k in range(scalars):
        send[COEFS + k : COEFS + k + 1, :] = tree_sum([got[j, COLS + k] for j in range(NG)])


def fold1_kernel(got, leaf_part, send, zero, one):
    fold_rows(got, 1, send, zero, one)
    send[COEFS + 1 :, :] = leaf_part[...]


def fold2_kernel(got, send, zero, one):
    fold_rows(got, 2, send, zero, one)


def send_rows(send, coefs, rows):
    send[0:COLS, :] = coefs
    for k, row in enumerate(rows):
        send[COLS + k : COLS + k + 1, :] = row


def sum_rows(got, scalars, held):
    for y in range(4):
        for r in range(COEFS):
            held[y, r : r + 1, :] = tree_sum([got[4 * y + x, r] for x in range(4)])
    table = [held[y, 0:COLS] for y in range(4)] + [unpack_half(held[y, COLS:COEFS]) for y in range(4)]
    return table, [tree_sum([got[j, COEFS + k] for j in range(NG)]) for k in range(scalars)]


def column_directions(marks, table, leaf_parts, got0, directions):
    low = lane((COLS, PTS)) < RANK
    odd = marks[NG : NG + 1, :] > 0.5
    top = tree_sum(table[0:4])
    for y in range(4):
        coefs = jnp.where(low, top, jnp.where(odd, table[4 + y], table[y]))
        high = coefs.astype(BF16)
        both = jnp.concatenate([high, (coefs - high.astype(F32)).astype(BF16)], 0)
        for j in range(4 * y, 4 * y + 4):
            bases = got0[j, BASES]
            first = bases.astype(BF16)
            r = jnp.dot(both, first, preferred_element_type=F32)
            r = r[0:COLS] + r[COLS:] + jnp.dot(high, (bases - first.astype(F32)).astype(BF16), preferred_element_type=F32)
            directions[j] = leaf_parts(j) + r


def own_direction(marks, directions):
    return tree_sum([directions[j] * marks[j : j + 1, :] for j in range(NG)])


def features(x, left):
    def pieces(v):
        first = v.astype(BF16).astype(F32)
        second = (v - first).astype(BF16).astype(F32)
        third = (v - first - second).astype(BF16).astype(F32)
        return first, second, third

    a, b, c = pieces(x)
    norms = pieces(jnp.sum(x * x, 0, keepdims=True))
    ones = (jnp.ones((1, PTS), F32),) * 3
    if left:
        parts = [a, a, b, b, a, c]
        tail = tile_rows(norms + ones)
    else:
        a, b, c = -2.0 * a, -2.0 * b, -2.0 * c
        parts = [a, b, a, b, c, a]
        tail = tile_rows(ones + norms)
    return jnp.concatenate(parts + [tail, jnp.zeros((PTS - 6 * COLS - 8, PTS), F32)], 0)


def first_kernel(marks, got_a, got_b, high, low, out, z, table, directions, left_f, right_f, both):
    tops = [tree_sum([got_a[4 * y + x, COLS : 2 * COLS] for x in range(4)]) for y in range(4)]
    subs = [tree_sum([got_a[4 * y + x, 2 * COLS : 5 * COLS // 2] for x in range(4)]) for y in range(4)]
    now = tops + [unpack_half(v) for v in subs]
    for t in range(NT):
        table[t] = now[t]
    column_directions(marks, now, lambda j: got_a[j, LEAF_PART], got_a, directions)
    z[...] = own_direction(marks, directions)
    for j in range(NG):
        at = slice(j * PTS, (j + 1) * PTS)
        right_f[:, at] = features(got_b[j, 0:COLS] * COORD_SCALE, False).astype(BF16)
        left_f[at, :] = features(got_a[j, 0:COLS] * COORD_SCALE, True).T.astype(BF16)
        v = directions[j] * LEAD
        v_high = v.astype(BF16)
        both[j] = jnp.concatenate([v_high, (v - v_high.astype(F32)).astype(BF16)], 0)
    points = left_f[...]
    vectors = jnp.concatenate([both[j] for j in range(NG)], 1)
    width = 256
    for j in range(0, NG * PTS, width):
        s = jnp.dot(points, right_f[:, j : j + width], preferred_element_type=F32)
        s = jnp.maximum(s, 1e-30)
        v = s * lax.rsqrt(s)
        w = v + SHIFT
        k = (w * w + REST) * jnp.exp2(-v)
        k_high = k.astype(BF16)
        k_low = (k - k_high.astype(F32)).astype(BF16)
        high[:, j : j + width] = k_high
        low[:, j : j + width] = k_low
        r = jnp.dot(vectors, k_high, preferred_element_type=F32)
        r = r[0:COLS] + r[COLS:] + jnp.dot(vectors[0:COLS], k_low, preferred_element_type=F32)
        for b in range(width // PTS):
            out[j // PTS + b] = r[:, b * PTS : (b + 1) * PTS]


def matvec(directions, high, low, out):
    v = jnp.concatenate([directions[j] * LEAD for j in range(NG)], 1)
    v_high = v.astype(BF16)
    both = jnp.concatenate([v_high, (v - v_high.astype(F32)).astype(BF16)], 0)
    width = 512
    for j in range(0, NG * PTS, width):
        r = jnp.dot(both, high[:, j : j + width], preferred_element_type=F32)
        r = r[0:COLS] + r[COLS:] + jnp.dot(v_high, low[:, j : j + width], preferred_element_type=F32)
        for b in range(width // PTS):
            out[j // PTS + b] = r[:, b * PTS : (b + 1) * PTS]


def image0_kernel(got, z, rhs, basis, leaf, q, leaf_part, send):
    q[...] = tree_sum([got[j] for j in range(NG)]) + NOISE * z[...]
    send_rows(send, dot_nt(q[...], basis[...]), [pack([rowdot(rhs[...], z[...]), rowdot(z[...], q[...])])])
    leaf_part[...] = dot_nt(q[...], leaf[...])


def second_kernel(
    marks, got, got0, table0, rhs, q, leaf_rhs, leaf_q, high, low,
    out, z, res, leaf_res, table, table_q, sums, directions, held, leaf_parts,
):
    now, (total,) = sum_rows(got, 1, held)
    for j in range(NG):
        for r in range(COLS):
            leaf_parts[j, r : r + 1, :] = got[j, COEFS + 1 + r]
    sums[...] = total
    alpha = unpack(total, 0) / unpack(total, 1)
    for t in range(NT):
        table_q[t] = now[t]
        now[t] = table0[t] - alpha * now[t]
        table[t] = now[t]
    column_directions(
        marks, now, lambda j: got0[j, LEAF_PART] - alpha * leaf_parts[j], got0, directions
    )
    z[...] = own_direction(marks, directions)
    res[...] = rhs[...] - alpha * q[...]
    leaf_res[...] = leaf_rhs[...] - alpha * leaf_q[...]
    matvec(directions, high, low, out)


def image1_kernel(got, z1, z0, res, q, leaf_res, leaf_q, leaf, basis, p, send):
    p[...] = tree_sum([got[j] for j in range(NG)]) + NOISE * z1[...]
    rv, qv, pv, zv = res[...], q[...], p[...], z1[...]
    rb, qb, pb = leaf_res[...], leaf_q[...], dot_nt(pv, leaf[...])
    rows = [
        pack(
            [
                rowdot(rv, zv), rowdot(zv, pv), rowdot(zv, qv), rowdot(z0[...], pv),
                rowdot(rv, rb), rowdot(rv, qb), rowdot(rv, pb), rowdot(qv, qb),
            ]
        ),
        pack([rowdot(qv, pb), rowdot(pv, pb)]),
    ]
    send_rows(send, dot_nt(pv, basis[...]), rows)


def finish_kernel(got, z0, z1, res, q, p, table1, table_q, sums0, x_out, r_out, coefs, held):
    now, (sums, more) = sum_rows(got, 2, held)
    rz0, z0q = unpack(sums0[...], 0), unpack(sums0[...], 1)
    rz1, z1p, z1q, z0p, rbr, rbq, rbp, qbq = (unpack(sums, k) for k in range(8))
    qbp, pbp = unpack(more, 0), unpack(more, 1)
    alpha0 = rz0 / z0q
    beta0 = rz1 / rz0
    alpha1 = rz1 / (z1p + beta0 * (z1q + z0p) + beta0 * beta0 * z0q)
    image = p[...] + beta0 * q[...]
    r_out[...] = res[...] - alpha1 * image
    x_out[...] = alpha0 * z0[...] + alpha1 * (z1[...] + beta0 * z0[...])
    leaf_part = (
        rbr
        - 2.0 * alpha1 * (rbp + beta0 * rbq)
        + alpha1 * alpha1 * (pbp + 2.0 * beta0 * qbp + beta0 * beta0 * qbq)
    )
    low = lane((COLS, PTS)) < RANK
    now = [table1[t] - alpha1 * (now[t] + beta0 * table_q[t]) for t in range(NT)]
    top = jnp.where(low, tree_sum(now[0:4]), 0.0)
    squares = top * top + tree_sum([jnp.where(low, 0.0, v * v) for v in now])
    beta1 = (leaf_part + jnp.sum(squares, 1, keepdims=True)) / rz1
    for k, v in enumerate((alpha0, alpha1, beta0, beta1)):
        coefs[k // 2, k % 2 : k % 2 + 1, :] = pack([v])[:, 0:COLS]


def gather(block, axes):
    return lax.all_to_all(jnp.broadcast_to(block[None], (NG,) + block.shape), axes, 0, 0, tiled=True)


def scatter(parts):
    return lax.all_to_all(parts, GB, 0, 0, tiled=True)


def on_device(points, inverse_length, target, probe_bits, leaf_inverse, top_basis, sub_basis):
    vec = ((COLS, PTS), F32)
    square = ((PTS, PTS), F32)
    table = ((NT, COLS, PTS), F32)
    block = ((NG * PTS, NG * PTS), BF16)
    parts = ((NG, COLS, PTS), F32)
    rows1 = ((COLS + 1, PTS), F32)
    rows2 = ((COLS + 2, PTS), F32)
    held = pltpu.VMEM((4, COEFS, PTS), F32)
    two = [pltpu.VMEM((COLS, PTS), F32)] * 2
    dma = pltpu.SemaphoreType.DMA
    where = lax.axis_index(("zl",) + GA).astype(jnp.int32).reshape(1)
    send, rhs, basis, leaf, leaf_part, marks = call(
        start_kernel,
        [((2 * COLS, PTS), F32), vec, square, square, vec, ((NG + 8, PTS), F32)],
        where, inverse_length, points, target[None, :], probe_bits, top_basis, sub_basis, leaf_inverse,
        spaces=[SMEM] + [HBM] * 7,
        scratch=[
            pltpu.VMEM((COLS, PTS), F32), pltpu.VMEM((1, PTS), F32), pltpu.VMEM((COLS - 1, PTS), jnp.int32),
            pltpu.SMEM((COLS,), F32), dma((7,)),
        ],
        name="start",
    )
    got_b = gather(send, GB)
    (send,) = call(fold0_kernel, [((SEND0, PTS), F32)], got_b, send, basis, leaf_part, name="fold0")
    got_a = gather(send, GA)
    high, low, out, z0, table0 = call(
        first_kernel, [block, block, parts, vec, table], marks, got_a, got_b, limit=24 << 20,
        scratch=[
            pltpu.VMEM((NG, COLS, PTS), F32), pltpu.VMEM((NG * PTS, PTS), BF16), pltpu.VMEM((PTS, NG * PTS), BF16),
            pltpu.VMEM((NG, 2 * COLS, PTS), BF16),
        ],
        name="first",
    )
    q, leaf_q, send = call(image0_kernel, [vec, vec, rows1], scatter(out), z0, rhs, basis, leaf, name="image0")
    (send,) = call(fold1_kernel, [((COEFS + 1 + COLS, PTS), F32)], gather(send[:, None], GB), leaf_q, scratch=two, name="fold1")
    out, z1, res, leaf_res, table1, table_q, sums0 = call(
        second_kernel, [parts, vec, vec, vec, table, table, ((1, PTS), F32)],
        marks, gather(send[:, None], GA), got_a, table0, rhs, q, leaf_part, leaf_q, high, low,
        limit=24 << 20,
        scratch=[pltpu.VMEM((NG, COLS, PTS), F32), held, pltpu.VMEM((NG, COLS, PTS), F32)], name="second",
    )
    p, send = call(
        image1_kernel, [vec, rows2], scatter(out), z1, z0, res, q, leaf_res, leaf_q, leaf, basis, name="image1"
    )
    (send,) = call(fold2_kernel, [((COEFS + 2, PTS), F32)], gather(send[:, None], GB), scratch=two, name="fold2")
    x_out, r_out, coefs = call(
        finish_kernel, [vec, vec, ((2, 2, COLS), F32)],
        gather(send[:, None], GA), z0, z1, res, q, p, table1, table_q, sums0,
        scratch=[held], name="finish",
    )
    return x_out, r_out, coefs


def solution(mesh):
    named = Mesh(mesh.devices.reshape(2, 4, 4, 4, 2), AXES)
    return jax.shard_map(
        on_device,
        mesh=named,
        in_specs=(P(None, AXES), P(), P(AXES), P(None, AXES), P(AXES, None), P(None, AXES), P(None, AXES)),
        out_specs=(P(None, AXES), P(None, AXES), P()),
        check_vma=False,
    )
```

```python
import functools
import math

import jax
import jax.numpy as jnp
from jax import lax
from jax.experimental import pallas as pl
from jax.experimental.pallas import tpu as pltpu
from jax.sharding import Mesh
from jax.sharding import PartitionSpec as P

AXES = ("zl", "y", "zh", "x", "c")
GA = ("y", "x")
GB = ("zl", "zh", "c")
NG = 16
NT = 8
COLS = 16
PTS = 128
RANK = 64
NOISE = 0.5
F32 = jnp.float32
BF16 = jnp.bfloat16
LN2 = math.log(2.0)
COORD_SCALE = math.sqrt(5.0) / LN2
LEAD = LN2 * LN2 / 3.0
SHIFT = 1.5 / LN2
REST = 1.0 / LEAD - SHIFT * SHIFT
HIGHEST = lax.Precision.HIGHEST


def dot_nt(a, b):
    return lax.dot_general(a, b, (((1,), (1,)), ((), ())), precision=HIGHEST, preferred_element_type=F32)


def dot_nn(a, b):
    return lax.dot_general(a, b, (((1,), (0,)), ((), ())), precision=HIGHEST, preferred_element_type=F32)


def lane(shape):
    return lax.broadcasted_iota(jnp.int32, shape, 1)


def sublane(shape):
    return lax.broadcasted_iota(jnp.int32, shape, 0)


def pack(sums):
    shape = (COLS, PTS)
    acc = jnp.zeros(shape, F32)
    for k, s in enumerate(sums):
        acc = jnp.where(lane(shape) == COLS * k + sublane(shape), jnp.broadcast_to(s, shape), acc)
    return jnp.sum(acc, 0, keepdims=True)


def unpack(row, k):
    shape = (COLS, PTS)
    hit = lane(shape) == COLS * k + sublane(shape)
    return jnp.sum(jnp.where(hit, jnp.broadcast_to(row, shape), 0.0), 1, keepdims=True)


def rowdot(a, b):
    return jnp.sum(a * b, 1, keepdims=True)


def tile_rows(rows):
    shape = (8, PTS)
    out = jnp.zeros(shape, F32)
    for k, r in enumerate(rows):
        out = jnp.where(sublane(shape) == k, jnp.broadcast_to(r, shape), out)
    return out


def tree_sum(terms):
    terms = list(terms)
    while len(terms) > 1:
        terms = [terms[i] + terms[i + 1] if i + 1 < len(terms) else terms[i] for i in range(0, len(terms), 2)]
    return terms[0]


VMEM = pltpu.MemorySpace.VMEM
SMEM = pltpu.MemorySpace.SMEM
HBM = pltpu.MemorySpace.HBM


def call(kernel, outs, *args, spaces=None, out_spaces=None, limit=8 << 20, scratch=(), name=None):
    spaces = spaces or [VMEM] * len(args)
    out_spaces = out_spaces or [VMEM] * len(outs)
    args = [pltpu.with_memory_space_constraint(a, m) if m is HBM else a for a, m in zip(args, spaces)]
    return pl.pallas_call(
        kernel,
        out_shape=[m(s, d) if m is HBM else jax.ShapeDtypeStruct(s, d) for m, (s, d) in zip(out_spaces, outs)],
        in_specs=[pl.BlockSpec(memory_space=m) for m in spaces],
        out_specs=[pl.BlockSpec(memory_space=m) for m in out_spaces],
        scratch_shapes=list(scratch),
        compiler_params=pltpu.CompilerParams(vmem_limit_bytes=limit),
        name=name,
    )(*args)


HALF = COLS // 2
COEFS = COLS + HALF
SEND0 = 5 * COLS // 2 + PTS + COLS
BASES = slice(5 * COLS // 2, 5 * COLS // 2 + PTS)
LEAF_PART = slice(SEND0 - COLS, SEND0)


def start_kernel(where, inv_h, points_h, target_h, bits_h, top_h, sub_h, leaf_h, send, rhs, basis, leaf, leaf_part, marks, points, target, bits, inv, sems):
    moves = [
        pltpu.make_async_copy(src, dst, sems.at[k])
        for k, (src, dst) in enumerate(
            [
                (bits_h, bits),
                (target_h, target),
                (top_h, basis.at[pl.ds(0, RANK)]),
                (sub_h, basis.at[pl.ds(RANK, RANK)]),
                (points_h, points),
                (inv_h, inv),
                (leaf_h, leaf),
            ]
        )
    ]
    for m in moves:
        m.start()
    row = sublane((NG + 8, PTS))
    place = where[0]
    hit = (row == lax.rem(place, NG)) | ((row >= NG) & (place >= NG))
    marks[...] = jnp.where(hit, 1.0, 0.0)
    for m in moves:
        m.wait()
    scale = jnp.zeros((COLS, PTS), F32)
    for k in range(COLS):
        scale = jnp.where(sublane((COLS, PTS)) == k, inv[k], scale)
    rhs[0:1, :] = target[...]
    rhs[1:COLS, :] = 2.0 * bits[...].astype(F32) - 1.0
    send[0:COLS, :] = points[...] * scale
    send[COLS : 2 * COLS, :] = dot_nt(rhs[...], basis[...])
    leaf_part[...] = dot_nt(rhs[...], leaf[...])


def pack_half(tile):
    return jnp.where(lane((8, PTS)) < RANK, pltpu.roll(tile[0:8], RANK, 1), tile[8:16])


def unpack_half(packed):
    return jnp.concatenate([pltpu.roll(packed, RANK, 1), packed], 0)


def fold0_kernel(got, own, basis, leaf_part, send):
    low = lane((COLS, PTS)) < RANK
    zero = tree_sum([got[j, COLS : 2 * COLS] for j in range(NG // 2)])
    one = tree_sum([got[j, COLS : 2 * COLS] for j in range(NG // 2, NG)])
    send[0:COLS, :] = own[0:COLS, :]
    send[COLS : 2 * COLS, :] = jnp.where(low, zero + one, zero)
    send[2 * COLS : 5 * COLS // 2, :] = pack_half(one)
    send[BASES, :] = basis[...]
    send[LEAF_PART, :] = leaf_part[...]


def fold_rows(got, scalars, send, zero, one):
    for r in range(COLS):
        zero[r : r + 1, :] = tree_sum([got[j, r] for j in range(NG // 2)])
        one[r : r + 1, :] = tree_sum([got[j, r] for j in range(NG // 2, NG)])
    low = lane((COLS, PTS)) < RANK
    send[0:COLS, :] = jnp.where(low, zero[...] + one[...], zero[...])
    send[COLS:COEFS, :] = pack_half(one[...])
    for k in range(scalars):
        send[COEFS + k : COEFS + k + 1, :] = tree_sum([got[j, COLS + k] for j in range(NG)])


def fold1_kernel(got, leaf_part, send, zero, one):
    fold_rows(got, 1, send, zero, one)
    send[COEFS + 1 :, :] = leaf_part[...]


def fold2_kernel(got, send, zero, one):
    fold_rows(got, 1, send, zero, one)


def send_rows(send, coefs, rows):
    send[0:COLS, :] = coefs
    for k, row in enumerate(rows):
        send[COLS + k : COLS + k + 1, :] = row


def sum_rows(got, scalars, held):
    for y in range(4):
        for r in range(COEFS):
            held[y, r : r + 1, :] = tree_sum([got[4 * y + x, r] for x in range(4)])
    table = [held[y, 0:COLS] for y in range(4)] + [unpack_half(held[y, COLS:COEFS]) for y in range(4)]
    return table, [tree_sum([got[j, COEFS + k] for j in range(NG)]) for k in range(scalars)]


def column_directions(marks, table, leaf_parts, bases_high, bases_low, directions):
    low = lane((COLS, PTS)) < RANK
    odd = marks[NG : NG + 1, :] > 0.5
    top = tree_sum(table[0:4])
    for y in range(4):
        coefs = jnp.where(low, top, jnp.where(odd, table[4 + y], table[y]))
        high = coefs.astype(BF16)
        both = jnp.concatenate([high, (coefs - high.astype(F32)).astype(BF16)], 0)
        for j in range(4 * y, 4 * y + 4):
            r = jnp.dot(both, bases_high[j], preferred_element_type=F32)
            r = r[0:COLS] + r[COLS:] + jnp.dot(high, bases_low[j], preferred_element_type=F32)
            directions[j] = leaf_parts(j) + r


def own_direction(marks, directions):
    return tree_sum([directions[j] * marks[j : j + 1, :] for j in range(NG)])


def features(x, left):
    def pieces(v):
        first = v.astype(BF16).astype(F32)
        second = (v - first).astype(BF16).astype(F32)
        third = (v - first - second).astype(BF16).astype(F32)
        return first, second, third

    a, b, c = pieces(x)
    norms = pieces(jnp.sum(x * x, 0, keepdims=True))
    ones = (jnp.ones((1, PTS), F32),) * 3
    if left:
        parts = [a, a, b, b, a, c]
        tail = tile_rows(norms + ones)
    else:
        a, b, c = -2.0 * a, -2.0 * b, -2.0 * c
        parts = [a, b, a, b, c, a]
        tail = tile_rows(ones + norms)
    return jnp.concatenate(parts + [tail, jnp.zeros((PTS - 6 * COLS - 8, PTS), F32)], 0)


def first_kernel(marks, got_a, got_b, high, low, out, z, table, bases_high, bases_low, directions, left_f, right_f, both):
    tops = [tree_sum([got_a[4 * y + x, COLS : 2 * COLS] for x in range(4)]) for y in range(4)]
    subs = [tree_sum([got_a[4 * y + x, 2 * COLS : 5 * COLS // 2] for x in range(4)]) for y in range(4)]
    now = tops + [unpack_half(v) for v in subs]
    for t in range(NT):
        table[t] = now[t]
    for j in range(NG):
        bases = got_a[j, BASES]
        bases_high[j] = bases.astype(BF16)
        bases_low[j] = (bases - bases.astype(BF16).astype(F32)).astype(BF16)
    column_directions(marks, now, lambda j: got_a[j, LEAF_PART], bases_high, bases_low, directions)
    z[...] = own_direction(marks, directions)
    for j in range(NG):
        at = slice(j * PTS, (j + 1) * PTS)
        right_f[:, at] = features(got_b[j, 0:COLS] * COORD_SCALE, False).astype(BF16)
        left_f[at, :] = features(got_a[j, 0:COLS] * COORD_SCALE, True).T.astype(BF16)
        v = directions[j] * LEAD
        v_high = v.astype(BF16)
        both[j] = jnp.concatenate([v_high, (v - v_high.astype(F32)).astype(BF16)], 0)
    points = left_f[...]
    vectors = jnp.concatenate([both[j] for j in range(NG)], 1)
    width = 256
    for j in range(0, NG * PTS, width):
        s = jnp.dot(points, right_f[:, j : j + width], preferred_element_type=F32)
        s = jnp.maximum(s, 1e-30)
        v = s * lax.rsqrt(s)
        w = v + SHIFT
        k = (w * w + REST) * jnp.exp2(-v)
        k_high = k.astype(BF16)
        k_low = (k - k_high.astype(F32)).astype(BF16)
        high[:, j : j + width] = k_high
        low[:, j : j + width] = k_low
        r = jnp.dot(vectors, k_high, preferred_element_type=F32)
        r = r[0:COLS] + r[COLS:] + jnp.dot(vectors[0:COLS], k_low, preferred_element_type=F32)
        for b in range(width // PTS):
            out[j // PTS + b] = r[:, b * PTS : (b + 1) * PTS]


def matvec(directions, high, low, out):
    v = jnp.concatenate([directions[j] * LEAD for j in range(NG)], 1)
    v_high = v.astype(BF16)
    both = jnp.concatenate([v_high, (v - v_high.astype(F32)).astype(BF16)], 0)
    width = 512
    for j in range(0, NG * PTS, width):
        r = jnp.dot(both, high[:, j : j + width], preferred_element_type=F32)
        r = r[0:COLS] + r[COLS:] + jnp.dot(v_high, low[:, j : j + width], preferred_element_type=F32)
        for b in range(width // PTS):
            out[j // PTS + b] = r[:, b * PTS : (b + 1) * PTS]


def image0_kernel(got, z, rhs, basis, leaf, q, leaf_part, send):
    q[...] = tree_sum([got[j] for j in range(NG)]) + NOISE * z[...]
    leaf_part[...] = dot_nt(q[...], leaf[...])
    send_rows(send, dot_nt(q[...], basis[...]), [
        pack([rowdot(rhs[...], z[...]), rowdot(z[...], q[...]), rowdot(q[...], leaf_part[...])])
    ])


def second_kernel(
    marks, got, got0, bases_high, bases_low, table0, rhs, q, leaf_rhs, leaf_q, high, low,
    out, z, res, leaf_res, table, table_q, sums, directions, held, leaf_parts,
):
    now, (total,) = sum_rows(got, 1, held)
    for j in range(NG):
        for r in range(COLS):
            leaf_parts[j, r : r + 1, :] = got[j, COEFS + 1 + r]
    sums[...] = total
    alpha = unpack(total, 0) / unpack(total, 1)
    for t in range(NT):
        table_q[t] = now[t]
        now[t] = table0[t] - alpha * now[t]
        table[t] = now[t]
    column_directions(
        marks, now, lambda j: got0[j, LEAF_PART] - alpha * leaf_parts[j], bases_high, bases_low, directions
    )
    z[...] = own_direction(marks, directions)
    res[...] = rhs[...] - alpha * q[...]
    leaf_res[...] = leaf_rhs[...] - alpha * leaf_q[...]
    matvec(directions, high, low, out)


def image1_kernel(got, z1, res, q, leaf_res, leaf_q, leaf, basis, p, send):
    p[...] = tree_sum([got[j] for j in range(NG)]) + NOISE * z1[...]
    rv, qv, pv, zv = res[...], q[...], p[...], z1[...]
    rb, qb, pb = leaf_res[...], leaf_q[...], dot_nt(pv, leaf[...])
    pairs = ((rv, zv), (zv, pv), (zv, qv), (rv, rb), (rv, qb), (rv, pb), (qv, pb), (pv, pb))
    rows = [pack([rowdot(a, b) for a, b in pairs])]
    send_rows(send, dot_nt(pv, basis[...]), rows)


def finish_kernel(got, z0, z1, res, q, p, table1, table_q, sums0, x_out, r_out, coefs, held):
    now, (sums,) = sum_rows(got, 1, held)
    rz0, z0q, qbq = (unpack(sums0[...], k) for k in range(3))
    rz1, z1p, z1q, rbr, rbq, rbp, qbp, pbp = (unpack(sums, k) for k in range(8))
    alpha0 = rz0 / z0q
    beta0 = rz1 / rz0
    alpha1 = rz1 / (z1p + 2.0 * beta0 * z1q + beta0 * beta0 * z0q)
    image = p[...] + beta0 * q[...]
    r_out[...] = res[...] - alpha1 * image
    x_out[...] = alpha0 * z0[...] + alpha1 * (z1[...] + beta0 * z0[...])
    leaf_part = (
        rbr
        - 2.0 * alpha1 * (rbp + beta0 * rbq)
        + alpha1 * alpha1 * (pbp + 2.0 * beta0 * qbp + beta0 * beta0 * qbq)
    )
    low = lane((COLS, PTS)) < RANK
    now = [table1[t] - alpha1 * (now[t] + beta0 * table_q[t]) for t in range(NT)]
    top = jnp.where(low, tree_sum(now[0:4]), 0.0)
    squares = top * top + tree_sum([jnp.where(low, 0.0, v * v) for v in now])
    beta1 = (leaf_part + jnp.sum(squares, 1, keepdims=True)) / rz1
    for k, v in enumerate((alpha0, alpha1, beta0, beta1)):
        coefs[k // 2, k % 2 : k % 2 + 1, :] = pack([v])[:, 0:COLS]


def gather(block, axes):
    return lax.all_to_all(jnp.broadcast_to(block[None], (NG,) + block.shape), axes, 0, 0, tiled=True)


def scatter(parts):
    return lax.all_to_all(parts, GB, 0, 0, tiled=True)


def on_device(points, inverse_length, target, probe_bits, leaf_inverse, top_basis, sub_basis):
    vec = ((COLS, PTS), F32)
    square = ((PTS, PTS), F32)
    table = ((NT, COLS, PTS), F32)
    block = ((NG * PTS, NG * PTS), BF16)
    parts = ((NG, COLS, PTS), F32)
    bases = ((NG, PTS, PTS), BF16)
    rows1 = ((COLS + 1, PTS), F32)
    held = pltpu.VMEM((4, COEFS, PTS), F32)
    two = [pltpu.VMEM((COLS, PTS), F32)] * 2
    dma = pltpu.SemaphoreType.DMA
    where = lax.axis_index(("zl",) + GA).astype(jnp.int32).reshape(1)
    send, rhs, basis, leaf, leaf_part, marks = call(
        start_kernel,
        [((2 * COLS, PTS), F32), vec, square, square, vec, ((NG + 8, PTS), F32)],
        where, inverse_length, points, target[None, :], probe_bits, top_basis, sub_basis, leaf_inverse,
        spaces=[SMEM] + [HBM] * 7,
        scratch=[
            pltpu.VMEM((COLS, PTS), F32), pltpu.VMEM((1, PTS), F32), pltpu.VMEM((COLS - 1, PTS), jnp.int32),
            pltpu.SMEM((COLS,), F32), dma((7,)),
        ],
        name="start",
    )
    got_b = gather(send, GB)
    (send,) = call(fold0_kernel, [((SEND0, PTS), F32)], got_b, send, basis, leaf_part, name="fold0")
    got_a = gather(send, GA)
    high, low, out, z0, table0, bases_high, bases_low = call(
        first_kernel, [block, block, parts, vec, table, bases, bases], marks, got_a, got_b, limit=24 << 20,
        scratch=[
            pltpu.VMEM((NG, COLS, PTS), F32), pltpu.VMEM((NG * PTS, PTS), BF16), pltpu.VMEM((PTS, NG * PTS), BF16),
            pltpu.VMEM((NG, 2 * COLS, PTS), BF16),
        ],
        name="first",
    )
    q, leaf_q, send = call(image0_kernel, [vec, vec, rows1], scatter(out), z0, rhs, basis, leaf, name="image0")
    (send,) = call(fold1_kernel, [((COEFS + 1 + COLS, PTS), F32)], gather(send[:, None], GB), leaf_q, scratch=two, name="fold1")
    out, z1, res, leaf_res, table1, table_q, sums0 = call(
        second_kernel, [parts, vec, vec, vec, table, table, ((1, PTS), F32)],
        marks, gather(send[:, None], GA), got_a, bases_high, bases_low, table0, rhs, q, leaf_part, leaf_q, high, low,
        limit=24 << 20,
        scratch=[pltpu.VMEM((NG, COLS, PTS), F32), held, pltpu.VMEM((NG, COLS, PTS), F32)], name="second",
    )
    p, send = call(
        image1_kernel, [vec, rows1], scatter(out), z1, res, q, leaf_res, leaf_q, leaf, basis, name="image1"
    )
    (send,) = call(fold2_kernel, [((COEFS + 1, PTS), F32)], gather(send[:, None], GB), scratch=two, name="fold2")
    x_out, r_out, coefs = call(
        finish_kernel, [vec, vec, ((2, 2, COLS), F32)],
        gather(send[:, None], GA), z0, z1, res, q, p, table1, table_q, sums0,
        scratch=[held], name="finish",
    )
    return x_out, r_out, coefs


def solution(mesh):
    named = Mesh(mesh.devices.reshape(2, 4, 4, 4, 2), AXES)
    return jax.shard_map(
        on_device,
        mesh=named,
        in_specs=(P(None, AXES), P(), P(AXES), P(None, AXES), P(AXES, None), P(None, AXES), P(None, AXES)),
        out_specs=(P(None, AXES), P(None, AXES), P()),
        check_vma=False,
    )
```

```python
import functools
import math

import jax
import jax.numpy as jnp
from jax import lax
from jax.experimental import pallas as pl
from jax.experimental.pallas import tpu as pltpu
from jax.sharding import Mesh
from jax.sharding import PartitionSpec as P

AXES = ("zl", "y", "zh", "x", "c")
GA = ("y", "x")
GB = ("zl", "zh", "c")
NG = 16
NT = 8
COLS = 16
PTS = 128
RANK = 64
NOISE = 0.5
F32 = jnp.float32
BF16 = jnp.bfloat16
LN2 = math.log(2.0)
COORD_SCALE = math.sqrt(5.0) / LN2
LEAD = LN2 * LN2 / 3.0
SHIFT = 1.5 / LN2
REST = 1.0 / LEAD - SHIFT * SHIFT
HIGHEST = lax.Precision.HIGHEST


def dot_nt(a, b):
    return lax.dot_general(a, b, (((1,), (1,)), ((), ())), precision=HIGHEST, preferred_element_type=F32)


def dot_nn(a, b):
    return lax.dot_general(a, b, (((1,), (0,)), ((), ())), precision=HIGHEST, preferred_element_type=F32)


def lane(shape):
    return lax.broadcasted_iota(jnp.int32, shape, 1)


def sublane(shape):
    return lax.broadcasted_iota(jnp.int32, shape, 0)


def pack(sums):
    shape = (COLS, PTS)
    acc = jnp.zeros(shape, F32)
    for k, s in enumerate(sums):
        acc = jnp.where(lane(shape) == COLS * k + sublane(shape), jnp.broadcast_to(s, shape), acc)
    return jnp.sum(acc, 0, keepdims=True)


def unpack(row, k):
    shape = (COLS, PTS)
    hit = lane(shape) == COLS * k + sublane(shape)
    return jnp.sum(jnp.where(hit, jnp.broadcast_to(row, shape), 0.0), 1, keepdims=True)


def rowdot(a, b):
    return jnp.sum(a * b, 1, keepdims=True)


def tile_rows(rows):
    shape = (8, PTS)
    out = jnp.zeros(shape, F32)
    for k, r in enumerate(rows):
        out = jnp.where(sublane(shape) == k, jnp.broadcast_to(r, shape), out)
    return out


def tree_sum(terms):
    terms = list(terms)
    while len(terms) > 1:
        terms = [terms[i] + terms[i + 1] if i + 1 < len(terms) else terms[i] for i in range(0, len(terms), 2)]
    return terms[0]


VMEM = pltpu.MemorySpace.VMEM
SMEM = pltpu.MemorySpace.SMEM
HBM = pltpu.MemorySpace.HBM


def call(kernel, outs, *args, spaces=None, out_spaces=None, limit=8 << 20, scratch=(), name=None):
    spaces = spaces or [VMEM] * len(args)
    out_spaces = out_spaces or [VMEM] * len(outs)
    args = [pltpu.with_memory_space_constraint(a, m) if m is HBM else a for a, m in zip(args, spaces)]
    return pl.pallas_call(
        kernel,
        out_shape=[m(s, d) if m is HBM else jax.ShapeDtypeStruct(s, d) for m, (s, d) in zip(out_spaces, outs)],
        in_specs=[pl.BlockSpec(memory_space=m) for m in spaces],
        out_specs=[pl.BlockSpec(memory_space=m) for m in out_spaces],
        scratch_shapes=list(scratch),
        compiler_params=pltpu.CompilerParams(vmem_limit_bytes=limit),
        name=name,
    )(*args)


HALF = COLS // 2
COEFS = COLS + HALF
SEND0 = 5 * COLS // 2 + PTS + COLS
BASES = slice(5 * COLS // 2, 5 * COLS // 2 + PTS)
LEAF_PART = slice(SEND0 - COLS, SEND0)


def start_kernel(where, inv_h, points_h, target_h, bits_h, top_h, sub_h, leaf_h, send, rhs, weights, leaf_part, marks, points, target, bits, inv, sems):
    moves = [
        pltpu.make_async_copy(src, dst, sems.at[k])
        for k, (src, dst) in enumerate(
            [
                (bits_h, bits),
                (target_h, target),
                (top_h, weights.at[pl.ds(0, RANK)]),
                (sub_h, weights.at[pl.ds(RANK, RANK)]),
                (points_h, points),
                (inv_h, inv),
                (leaf_h, weights.at[pl.ds(PTS, PTS)]),
            ]
        )
    ]
    for m in moves:
        m.start()
    row = sublane((NG + 8, PTS))
    place = where[0]
    hit = (row == lax.rem(place, NG)) | ((row >= NG) & (place >= NG))
    marks[...] = jnp.where(hit, 1.0, 0.0)
    for m in moves:
        m.wait()
    scale = jnp.zeros((COLS, PTS), F32)
    for k in range(COLS):
        scale = jnp.where(sublane((COLS, PTS)) == k, inv[k], scale)
    rhs[0:1, :] = target[...]
    rhs[1:COLS, :] = 2.0 * bits[...].astype(F32) - 1.0
    send[0:COLS, :] = points[...] * scale
    both = dot_nt(rhs[...], weights[...])
    send[COLS : 2 * COLS, :] = both[:, 0:PTS]
    leaf_part[...] = both[:, PTS:]


def pack_half(tile):
    return jnp.where(lane((8, PTS)) < RANK, pltpu.roll(tile[0:8], RANK, 1), tile[8:16])


def unpack_half(packed):
    return jnp.concatenate([pltpu.roll(packed, RANK, 1), packed], 0)


def fold0_kernel(got, own, weights, leaf_part, send):
    low = lane((COLS, PTS)) < RANK
    zero = tree_sum([got[j, COLS : 2 * COLS] for j in range(NG // 2)])
    one = tree_sum([got[j, COLS : 2 * COLS] for j in range(NG // 2, NG)])
    send[0:COLS, :] = own[0:COLS, :]
    send[COLS : 2 * COLS, :] = jnp.where(low, zero + one, zero)
    send[2 * COLS : 5 * COLS // 2, :] = pack_half(one)
    send[BASES, :] = weights[0:PTS, :]
    send[LEAF_PART, :] = leaf_part[...]


def fold_rows(got, scalars, send, zero, one):
    for r in range(COLS):
        zero[r : r + 1, :] = tree_sum([got[j, r] for j in range(NG // 2)])
        one[r : r + 1, :] = tree_sum([got[j, r] for j in range(NG // 2, NG)])
    low = lane((COLS, PTS)) < RANK
    send[0:COLS, :] = jnp.where(low, zero[...] + one[...], zero[...])
    send[COLS:COEFS, :] = pack_half(one[...])
    for k in range(scalars):
        send[COEFS + k : COEFS + k + 1, :] = tree_sum([got[j, COLS + k] for j in range(NG)])


def fold1_kernel(got, leaf_part, send, zero, one):
    fold_rows(got, 1, send, zero, one)
    send[COEFS + 1 :, :] = leaf_part[...]


def fold2_kernel(got, send, zero, one):
    fold_rows(got, 1, send, zero, one)


def send_rows(send, coefs, rows):
    send[0:COLS, :] = coefs
    for k, row in enumerate(rows):
        send[COLS + k : COLS + k + 1, :] = row


def sum_rows(got, scalars, held):
    for y in range(4):
        for r in range(COEFS):
            held[y, r : r + 1, :] = tree_sum([got[4 * y + x, r] for x in range(4)])
    table = [held[y, 0:COLS] for y in range(4)] + [unpack_half(held[y, COLS:COEFS]) for y in range(4)]
    return table, [tree_sum([got[j, COEFS + k] for j in range(NG)]) for k in range(scalars)]


def column_directions(marks, table, leaf_parts, bases_high, bases_low, directions):
    low = lane((COLS, PTS)) < RANK
    odd = marks[NG : NG + 1, :] > 0.5
    top = tree_sum(table[0:4])
    for y in range(4):
        coefs = jnp.where(low, top, jnp.where(odd, table[4 + y], table[y]))
        high = coefs.astype(BF16)
        both = jnp.concatenate([high, (coefs - high.astype(F32)).astype(BF16)], 0)
        for j in range(4 * y, 4 * y + 4):
            r = jnp.dot(both, bases_high[j], preferred_element_type=F32)
            r = r[0:COLS] + r[COLS:] + jnp.dot(high, bases_low[j], preferred_element_type=F32)
            directions[j] = leaf_parts(j) + r


def own_direction(marks, directions):
    return tree_sum([directions[j] * marks[j : j + 1, :] for j in range(NG)])


def features(x, left):
    def pieces(v):
        first = v.astype(BF16).astype(F32)
        second = (v - first).astype(BF16).astype(F32)
        third = (v - first - second).astype(BF16).astype(F32)
        return first, second, third

    a, b, c = pieces(x)
    norms = pieces(jnp.sum(x * x, 0, keepdims=True))
    ones = (jnp.ones((1, PTS), F32),) * 3
    if left:
        parts = [a, a, b, b, a, c]
        tail = tile_rows(norms + ones)
    else:
        a, b, c = -2.0 * a, -2.0 * b, -2.0 * c
        parts = [a, b, a, b, c, a]
        tail = tile_rows(ones + norms)
    return jnp.concatenate(parts + [tail, jnp.zeros((PTS - 6 * COLS - 8, PTS), F32)], 0)


def first_kernel(marks, got_a, got_b, high, low, out, z, table, bases_high, bases_low, directions, left_f, right_f, both):
    tops = [tree_sum([got_a[4 * y + x, COLS : 2 * COLS] for x in range(4)]) for y in range(4)]
    subs = [tree_sum([got_a[4 * y + x, 2 * COLS : 5 * COLS // 2] for x in range(4)]) for y in range(4)]
    now = tops + [unpack_half(v) for v in subs]
    for t in range(NT):
        table[t] = now[t]
    for j in range(NG):
        bases = got_a[j, BASES]
        bases_high[j] = bases.astype(BF16)
        bases_low[j] = (bases - bases.astype(BF16).astype(F32)).astype(BF16)
    column_directions(marks, now, lambda j: got_a[j, LEAF_PART], bases_high, bases_low, directions)
    z[...] = own_direction(marks, directions)
    for j in range(NG):
        at = slice(j * PTS, (j + 1) * PTS)
        right_f[:, at] = features(got_b[j, 0:COLS] * COORD_SCALE, False).astype(BF16)
        left_f[at, :] = features(got_a[j, 0:COLS] * COORD_SCALE, True).T.astype(BF16)
        v = directions[j] * LEAD
        v_high = v.astype(BF16)
        both[j] = jnp.concatenate([v_high, (v - v_high.astype(F32)).astype(BF16)], 0)
    points = left_f[...]
    vectors = jnp.concatenate([both[j] for j in range(NG)], 1)
    width = 256
    for j in range(0, NG * PTS, width):
        s = jnp.dot(points, right_f[:, j : j + width], preferred_element_type=F32)
        s = jnp.maximum(s, 1e-30)
        v = s * lax.rsqrt(s)
        w = v + SHIFT
        k = (w * w + REST) * jnp.exp2(-v)
        k_high = k.astype(BF16)
        k_low = (k - k_high.astype(F32)).astype(BF16)
        high[:, j : j + width] = k_high
        low[:, j : j + width] = k_low
        r = jnp.dot(vectors, k_high, preferred_element_type=F32)
        r = r[0:COLS] + r[COLS:] + jnp.dot(vectors[0:COLS], k_low, preferred_element_type=F32)
        for b in range(width // PTS):
            out[j // PTS + b] = r[:, b * PTS : (b + 1) * PTS]


def matvec(directions, high, low, out):
    v = jnp.concatenate([directions[j] * LEAD for j in range(NG)], 1)
    v_high = v.astype(BF16)
    both = jnp.concatenate([v_high, (v - v_high.astype(F32)).astype(BF16)], 0)
    width = 512
    for j in range(0, NG * PTS, width):
        r = jnp.dot(both, high[:, j : j + width], preferred_element_type=F32)
        r = r[0:COLS] + r[COLS:] + jnp.dot(v_high, low[:, j : j + width], preferred_element_type=F32)
        for b in range(width // PTS):
            out[j // PTS + b] = r[:, b * PTS : (b + 1) * PTS]


def image0_kernel(got, z, rhs, weights, q, leaf_part, send):
    q[...] = tree_sum([got[j] for j in range(NG)]) + NOISE * z[...]
    both = dot_nt(q[...], weights[...])
    leaf_part[...] = both[:, PTS:]
    send_rows(send, both[:, 0:PTS], [
        pack([rowdot(rhs[...], z[...]), rowdot(z[...], q[...]), rowdot(q[...], leaf_part[...])])
    ])


def second_kernel(
    marks, got, got0, bases_high, bases_low, table0, rhs, q, leaf_rhs, leaf_q, high, low,
    out, z, res, leaf_res, table, table_q, sums, directions, held, leaf_parts,
):
    now, (total,) = sum_rows(got, 1, held)
    for j in range(NG):
        for r in range(COLS):
            leaf_parts[j, r : r + 1, :] = got[j, COEFS + 1 + r]
    sums[...] = total
    alpha = unpack(total, 0) / unpack(total, 1)
    for t in range(NT):
        table_q[t] = now[t]
        now[t] = table0[t] - alpha * now[t]
        table[t] = now[t]
    column_directions(
        marks, now, lambda j: got0[j, LEAF_PART] - alpha * leaf_parts[j], bases_high, bases_low, directions
    )
    z[...] = own_direction(marks, directions)
    res[...] = rhs[...] - alpha * q[...]
    leaf_res[...] = leaf_rhs[...] - alpha * leaf_q[...]
    matvec(directions, high, low, out)


def image1_kernel(got, z1, res, q, leaf_res, leaf_q, weights, p, send):
    p[...] = tree_sum([got[j] for j in range(NG)]) + NOISE * z1[...]
    rv, qv, pv, zv = res[...], q[...], p[...], z1[...]
    both = dot_nt(pv, weights[...])
    rb, qb, pb = leaf_res[...], leaf_q[...], both[:, PTS:]
    pairs = ((rv, zv), (zv, pv), (zv, qv), (rv, rb), (rv, qb), (rv, pb), (qv, pb), (pv, pb))
    rows = [pack([rowdot(a, b) for a, b in pairs])]
    send_rows(send, both[:, 0:PTS], rows)


def finish_kernel(got, z0, z1, res, q, p, table1, table_q, sums0, x_out, r_out, coefs, held):
    now, (sums,) = sum_rows(got, 1, held)
    rz0, z0q, qbq = (unpack(sums0[...], k) for k in range(3))
    rz1, z1p, z1q, rbr, rbq, rbp, qbp, pbp = (unpack(sums, k) for k in range(8))
    alpha0 = rz0 / z0q
    beta0 = rz1 / rz0
    alpha1 = rz1 / (z1p + 2.0 * beta0 * z1q + beta0 * beta0 * z0q)
    image = p[...] + beta0 * q[...]
    r_out[...] = res[...] - alpha1 * image
    x_out[...] = alpha0 * z0[...] + alpha1 * (z1[...] + beta0 * z0[...])
    leaf_part = (
        rbr
        - 2.0 * alpha1 * (rbp + beta0 * rbq)
        + alpha1 * alpha1 * (pbp + 2.0 * beta0 * qbp + beta0 * beta0 * qbq)
    )
    low = lane((COLS, PTS)) < RANK
    now = [table1[t] - alpha1 * (now[t] + beta0 * table_q[t]) for t in range(NT)]
    top = jnp.where(low, tree_sum(now[0:4]), 0.0)
    squares = top * top + tree_sum([jnp.where(low, 0.0, v * v) for v in now])
    beta1 = (leaf_part + jnp.sum(squares, 1, keepdims=True)) / rz1
    for k, v in enumerate((alpha0, alpha1, beta0, beta1)):
        coefs[k // 2, k % 2 : k % 2 + 1, :] = pack([v])[:, 0:COLS]


def gather(block, axes):
    return lax.all_to_all(jnp.broadcast_to(block[None], (NG,) + block.shape), axes, 0, 0, tiled=True)


def scatter(parts):
    return lax.all_to_all(parts, GB, 0, 0, tiled=True)


def on_device(points, inverse_length, target, probe_bits, leaf_inverse, top_basis, sub_basis):
    vec = ((COLS, PTS), F32)
    table = ((NT, COLS, PTS), F32)
    block = ((NG * PTS, NG * PTS), BF16)
    parts = ((NG, COLS, PTS), F32)
    bases = ((NG, PTS, PTS), BF16)
    rows1 = ((COLS + 1, PTS), F32)
    held = pltpu.VMEM((4, COEFS, PTS), F32)
    two = [pltpu.VMEM((COLS, PTS), F32)] * 2
    dma = pltpu.SemaphoreType.DMA
    where = lax.axis_index(("zl",) + GA).astype(jnp.int32).reshape(1)
    send, rhs, weights, leaf_part, marks = call(
        start_kernel,
        [((2 * COLS, PTS), F32), vec, ((2 * PTS, PTS), F32), vec, ((NG + 8, PTS), F32)],
        where, inverse_length, points, target[None, :], probe_bits, top_basis, sub_basis, leaf_inverse,
        spaces=[SMEM] + [HBM] * 7,
        scratch=[
            pltpu.VMEM((COLS, PTS), F32), pltpu.VMEM((1, PTS), F32), pltpu.VMEM((COLS - 1, PTS), jnp.int32),
            pltpu.SMEM((COLS,), F32), dma((7,)),
        ],
        name="start",
    )
    got_b = gather(send, GB)
    (send,) = call(fold0_kernel, [((SEND0, PTS), F32)], got_b, send, weights, leaf_part, name="fold0")
    got_a = gather(send, GA)
    high, low, out, z0, table0, bases_high, bases_low = call(
        first_kernel, [block, block, parts, vec, table, bases, bases], marks, got_a, got_b, limit=24 << 20,
        scratch=[
            pltpu.VMEM((NG, COLS, PTS), F32), pltpu.VMEM((NG * PTS, PTS), BF16), pltpu.VMEM((PTS, NG * PTS), BF16),
            pltpu.VMEM((NG, 2 * COLS, PTS), BF16),
        ],
        name="first",
    )
    q, leaf_q, send = call(image0_kernel, [vec, vec, rows1], scatter(out), z0, rhs, weights, name="image0")
    (send,) = call(fold1_kernel, [((COEFS + 1 + COLS, PTS), F32)], gather(send[:, None], GB), leaf_q, scratch=two, name="fold1")
    out, z1, res, leaf_res, table1, table_q, sums0 = call(
        second_kernel, [parts, vec, vec, vec, table, table, ((1, PTS), F32)],
        marks, gather(send[:, None], GA), got_a, bases_high, bases_low, table0, rhs, q, leaf_part, leaf_q, high, low,
        limit=24 << 20,
        scratch=[pltpu.VMEM((NG, COLS, PTS), F32), held, pltpu.VMEM((NG, COLS, PTS), F32)], name="second",
    )
    p, send = call(
        image1_kernel, [vec, rows1], scatter(out), z1, res, q, leaf_res, leaf_q, weights, name="image1"
    )
    (send,) = call(fold2_kernel, [((COEFS + 1, PTS), F32)], gather(send[:, None], GB), scratch=two, name="fold2")
    x_out, r_out, coefs = call(
        finish_kernel, [vec, vec, ((2, 2, COLS), F32)],
        gather(send[:, None], GA), z0, z1, res, q, p, table1, table_q, sums0,
        scratch=[held], name="finish",
    )
    return x_out, r_out, coefs


def solution(mesh):
    named = Mesh(mesh.devices.reshape(2, 4, 4, 4, 2), AXES)
    return jax.shard_map(
        on_device,
        mesh=named,
        in_specs=(P(None, AXES), P(), P(AXES), P(None, AXES), P(AXES, None), P(None, AXES), P(None, AXES)),
        out_specs=(P(None, AXES), P(None, AXES), P()),
        check_vma=False,
    )
```
